512 devices in a mesh: ex: 32 (over y_hi, x, core), feat: 16 (over z, y_lo).
Axes of the slice: x: 4, y: 8 (y_hi: 4, y_lo: 2; y = y_hi * 2 + y_lo), z: 8, core: 2. Of those that a mesh axis runs over, the one named last changes fastest.
Arguments:
- train_grads: bfloat16 [32768, 16384], P('ex', 'feat'), may hold values from -200 to 200
- target_grads: bfloat16 [512, 16384], P('ex', 'feat'), may hold values from -300 to 300
- target_mass: float32 [512], replicated, may hold values from 0.25 to 4
Outputs:
- mixtures: bfloat16 [512, 16384], P('ex', 'feat')
The draws below stay inside these ranges and needn't reach their ends.
All inputs are finite; a program needn't handle non-finite values.
Results may differ from the reference program's by a relative error of at most 0.0048.
Values may be sent and summed in bfloat16 or wider, within the bound.
No kernel may reach another device: no remote copies, remote signals or barrier semaphores. Data moves between devices by JAX's collectives and lax.ppermute only.
A program may use at most 64 MiB of HBM per device.

```python
import math
import jax
import jax.numpy as jnp
from jax import lax

F = 16384
ITERS = 3
NTR = 32768
NT = 512


def draw_pair(key):
    base = jax.random.fold_in(key, 11)
    keys = jax.random.split(base, 2)
    train = jnp.clip(jax.random.normal(keys[0], (NTR, F), jnp.float32), -6.0, 6.0)
    target = jnp.clip(jax.random.normal(keys[1], (NT, F), jnp.float32), -6.0, 6.0)
    return (train, target)


def draw_train_grads(key, part):
    return draw_pair(key)[0].astype(jnp.bfloat16)


def draw_target_grads(key, part):
    return draw_pair(key)[1].astype(jnp.bfloat16)


def setup_inputs(seed: int = 0) -> dict:
    arg_keys = jax.random.split(jax.random.key(seed), 4)
    train_grads = draw_train_grads(jax.random.fold_in(arg_keys[3], 71), 0)
    target_grads = draw_target_grads(jax.random.fold_in(arg_keys[3], 71), 0)
    target_mass = jnp.clip(jnp.exp(jax.random.uniform(arg_keys[2], (NT,), jnp.float32, math.log(0.25), math.log(4.0))), 0.25, 4.0)
    return dict(train_grads=train_grads, target_grads=target_grads, target_mass=target_mass)


def log_sum_exp(values, axis):
    top = lax.optimization_barrier(jnp.max(values, axis=axis, keepdims=True))
    total = lax.optimization_barrier(jnp.sum(jnp.exp(values - top), axis=axis))
    return jnp.squeeze(top, axis) + jnp.log(total)

def reference(train_grads, target_grads, target_mass):
    scale = 3.0 / math.sqrt(F)
    logits = jnp.dot(train_grads, target_grads.T, preferred_element_type=jnp.float32) * scale
    mass_total = jnp.sum(target_mass)
    weights = target_mass / mass_total
    log_b = jnp.log(target_mass) - jnp.log(mass_total)
    log_a = -math.log(NTR)
    col_pot = jnp.zeros((NT,), jnp.float32)
    row_pot = jnp.zeros((NTR,), jnp.float32)
    for step in range(ITERS):
        row_pot = log_a - log_sum_exp(logits + col_pot[None, :], 1)
        col_pot = log_b - log_sum_exp(logits + row_pot[:, None], 0)
    plan = jnp.exp(logits + row_pot[:, None] + col_pot[None, :]).astype(jnp.bfloat16)
    mixed = jnp.dot(plan.T, train_grads, preferred_element_type=jnp.float32)
    return (mixed / weights[:, None]).astype(jnp.bfloat16)
```

```python
import math

import jax
import jax.numpy as jnp
from jax import lax
from jax.sharding import Mesh, PartitionSpec as P

F = 16384
CHIPS = ("yh", "x")
EX = ("yh", "x", "c")
FEAT = ("z", "yl")


def split3(v):
    hi = lax.reduce_precision(v, 8, 7)
    rest = v - hi
    mid = lax.reduce_precision(rest, 8, 7)
    return hi, mid, rest - mid


def spread(block, axes, n):
    copies = jnp.broadcast_to(block[None], (n,) + block.shape)
    return lax.all_to_all(copies, axes, 0, 0, tiled=True)


def shards(train, target, mass):
    rows, feats = train.shape
    nc = lax.axis_size("c")
    nchips = lax.axis_size(CHIPS)
    nex = nc * nchips
    nf = lax.axis_size(FEAT)
    mine = target.shape[0]
    nt = mine * nex
    sub = rows // nf
    scale = 3.0 / math.sqrt(F)
    a = 1.0 / (rows * nex)

    same_core = spread(target, CHIPS, nchips).reshape(nchips * mine, feats)
    targets = spread(same_core, "c", nc).reshape(nt, feats)
    mass = mass.reshape(nchips, nc, mine).transpose(1, 0, 2).reshape(nt)
    b = mass / jnp.sum(mass)

    partial = lax.dot_general(
        train, targets, (((1,), (1,)), ((), ())), preferred_element_type=jnp.float32
    )
    parts = lax.all_to_all(partial.reshape(nf, sub, nt), FEAT, 0, 0, tiled=True)
    logits = jnp.sum(parts, axis=0) * scale

    top = jnp.max(logits, axis=1, keepdims=True)
    total = jnp.sum(jnp.exp(logits - top), axis=1, keepdims=True)
    v = logits - top - jnp.log(total)
    shift = jnp.max(v, axis=0)
    kern = jnp.exp(v - shift[None, :]).astype(jnp.bfloat16)
    tail = jnp.stack(split3(shift)).astype(jnp.bfloat16)
    tail = jnp.concatenate([tail, jnp.zeros((5, nt), jnp.bfloat16)], axis=0)
    block = jnp.concatenate([kern, tail], axis=0)
    blocks = spread(block, FEAT, nf).reshape(nf, sub + 8, nt)
    kern = blocks[:, :sub].astype(jnp.float32)
    shifts = jnp.sum(blocks[:, sub : sub + 3].astype(jnp.float32), axis=1)

    near = jnp.max(shifts, axis=0)
    near_sum = jnp.sum(jnp.exp(shifts - near[None]) * jnp.sum(kern, axis=1), axis=0)
    pairs = spread(jnp.stack([near, near_sum]), EX, nex).reshape(nex, 2, nt)
    far = jnp.max(pairs[:, 0], axis=0)
    far_sum = jnp.sum(jnp.exp(pairs[:, 0] - far[None]) * pairs[:, 1], axis=0)
    factor = jnp.exp(shifts - far[None]) * (b / far_sum)[None]
    plan = kern * factor[:, None, :]

    row = a / jnp.sum(plan, axis=2, keepdims=True)
    cols = jnp.sum(plan * row, axis=(0, 1))
    col = b / jnp.sum(spread(cols[None], EX, nex).reshape(nex, nt), axis=0)

    plan = plan * col[None, None, :]
    row = a / jnp.sum(plan, axis=2, keepdims=True)
    plan = plan * row
    cols = jnp.sum(plan, axis=(0, 1))
    cols = cols + lax.ppermute(cols, "c", [(0, 1), (1, 0)])
    plan = plan.astype(jnp.bfloat16).reshape(rows, nt)

    mixed = lax.dot_general(
        plan, train, (((0,), (0,)), ((), ())), preferred_element_type=jnp.float32
    )
    half = nt // nc
    halves = lax.all_to_all(mixed.reshape(nc, half, feats), "c", 0, 0, tiled=True)
    mixed = jnp.sum(halves, axis=0)
    my_cols = lax.dynamic_slice_in_dim(cols, lax.axis_index("c") * half, half)
    hi, mid, lo = split3(my_cols)
    lane = lax.broadcasted_iota(jnp.int32, (half, 128), 1)
    tail = jnp.where(lane == 0, hi[:, None], jnp.where(lane == 1, mid[:, None], lo[:, None]))
    send = jnp.concatenate([mixed, tail], axis=1).astype(jnp.bfloat16)
    got = lax.all_to_all(
        send.reshape(nchips, mine, feats + 128), CHIPS, 0, 0, tiled=True
    )
    got = jnp.sum(got.astype(jnp.float32), axis=0)
    mass_in = jnp.sum(got[:, feats : feats + 3], axis=1, keepdims=True)
    return (got[:, :feats] / mass_in).astype(jnp.bfloat16)


def solution(mesh):
    fine = Mesh(mesh.devices.reshape(4, 4, 2, 8, 2), ("yh", "x", "c", "z", "yl"))
    return jax.shard_map(
        shards,
        mesh=fine,
        in_specs=(P(EX, FEAT), P(EX, FEAT), P()),
        out_specs=P(EX, FEAT),
        check_vma=False,
    )
```

```python
import math

import jax
import jax.numpy as jnp
from jax import lax
from jax.sharding import Mesh, PartitionSpec as P

F = 16384
CHIPS = ("yh", "x")
EX = ("yh", "x", "c")
FEAT = ("z", "yl")
PIECES = ("yl", "z")
ROWS = ("yh", "x", "c", "yl")


def split3(v):
    hi = lax.reduce_precision(v, 8, 7)
    rest = v - hi
    mid = lax.reduce_precision(rest, 8, 7)
    return hi, mid, rest - mid


def spread(block, axes, n):
    copies = jnp.broadcast_to(block[None], (n,) + block.shape)
    return lax.all_to_all(copies, axes, 0, 0, tiled=True)


def shards(train, target, mass):
    rows, feats = train.shape
    nc = lax.axis_size("c")
    nchips = lax.axis_size(CHIPS)
    nex = nc * nchips
    nz = lax.axis_size("z")
    nf = lax.axis_size(FEAT)
    mine = target.shape[0]
    nt = mine * nex
    sub = rows // nf
    scale = 3.0 / math.sqrt(F)
    a = 1.0 / (rows * nex)

    same_core = spread(target, CHIPS, nchips).reshape(nchips * mine, feats)
    targets = spread(same_core, "c", nc).reshape(nt, feats)
    mass = mass.reshape(nchips, nc, mine).transpose(1, 0, 2).reshape(nt)
    b = mass / jnp.sum(mass)

    partial = lax.dot_general(
        train, targets, (((1,), (1,)), ((), ())), preferred_element_type=jnp.float32
    )
    parts = lax.all_to_all(partial.reshape(nf, sub, nt), PIECES, 0, 0, tiled=True)
    logits = jnp.sum(parts, axis=0) * scale

    top = jnp.max(logits, axis=1, keepdims=True)
    total = jnp.sum(jnp.exp(logits - top), axis=1, keepdims=True)
    v = logits - top - jnp.log(total)
    shift = jnp.max(v, axis=0)
    kern = jnp.exp(v - shift[None, :]).astype(jnp.bfloat16)
    tail = jnp.stack(split3(shift)).astype(jnp.bfloat16)
    tail = jnp.concatenate([tail, jnp.zeros((5, nt), jnp.bfloat16)], axis=0)
    block = jnp.concatenate([kern, tail], axis=0)
    blocks = spread(block, "z", nz).reshape(nz, sub + 8, nt)
    others = lax.ppermute(blocks, "yl", [(0, 1), (1, 0)])

    def unpack(blocks):
        kern = blocks[:, :sub].astype(jnp.float32)
        return kern, jnp.sum(blocks[:, sub : sub + 3].astype(jnp.float32), axis=1)

    kern, shifts = unpack(blocks)

    nrows = nex * lax.axis_size("yl")
    near = jnp.max(shifts, axis=0)
    near_sum = jnp.sum(jnp.exp(shifts - near[None]) * jnp.sum(kern, axis=1), axis=0)
    pairs = spread(jnp.stack([near, near_sum]), ROWS, nrows).reshape(nrows, 2, nt)
    far = jnp.max(pairs[:, 0], axis=0)
    far_sum = jnp.sum(jnp.exp(pairs[:, 0] - far[None]) * pairs[:, 1], axis=0)
    col = b / far_sum
    plan = kern * (jnp.exp(shifts - far[None]) * col[None])[:, None, :]

    row = a / jnp.sum(plan, axis=2, keepdims=True)
    cols = jnp.sum(plan * row, axis=(0, 1))
    col = col * (b / jnp.sum(spread(cols[None], ROWS, nrows).reshape(nrows, nt), axis=0))

    def third(kern, shifts):
        plan = kern * (jnp.exp(shifts - far[None]) * col[None])[:, None, :]
        plan = plan * (a / jnp.sum(plan, axis=2, keepdims=True))
        return plan.astype(jnp.bfloat16).reshape(nz * sub, nt), jnp.sum(plan, axis=(0, 1))

    plan, cols = third(kern, shifts)
    other_plan, other_cols = third(*unpack(others))
    cols = cols + other_cols
    cols = cols + lax.ppermute(cols, "c", [(0, 1), (1, 0)])

    yl = lax.axis_index("yl")
    mixed = sum(
        lax.dot_general(
            p,
            lax.dynamic_slice_in_dim(train, side * (nz * sub), nz * sub),
            (((0,), (0,)), ((), ())),
            preferred_element_type=jnp.float32,
        )
        for p, side in ((plan, yl), (other_plan, 1 - yl))
    )
    half = nt // nc
    halves = lax.all_to_all(mixed.reshape(nc, half, feats), "c", 0, 0, tiled=True)
    mixed = jnp.sum(halves, axis=0)
    my_cols = lax.dynamic_slice_in_dim(cols, lax.axis_index("c") * half, half)
    hi, mid, lo = split3(my_cols)
    lane = lax.broadcasted_iota(jnp.int32, (half, 128), 1)
    tail = jnp.where(lane == 0, hi[:, None], jnp.where(lane == 1, mid[:, None], lo[:, None]))
    send = jnp.concatenate([mixed, tail], axis=1).astype(jnp.bfloat16)
    got = lax.all_to_all(
        send.reshape(nchips, mine, feats + 128), CHIPS, 0, 0, tiled=True
    )
    got = jnp.sum(got.astype(jnp.float32), axis=0)
    mass_in = jnp.sum(got[:, feats : feats + 3], axis=1, keepdims=True)
    return (got[:, :feats] / mass_in).astype(jnp.bfloat16)


def solution(mesh):
    fine = Mesh(mesh.devices.reshape(4, 4, 2, 8, 2), ("yh", "x", "c", "z", "yl"))
    return jax.shard_map(
        shards,
        mesh=fine,
        in_specs=(P(EX, FEAT), P(EX, FEAT), P()),
        out_specs=P(EX, FEAT),
        check_vma=False,
    )
```

```python
import functools
import math

import jax
import jax.numpy as jnp
from jax import lax
from jax.experimental import pallas as pl
from jax.experimental.pallas import tpu as pltpu
from jax.sharding import Mesh, PartitionSpec as P


F = 16384
CHIPS = ("yh", "x")
EX = ("yh", "x", "c")
FEAT = ("z", "yl")
PIECES = ("yl", "z")
ROWS = ("yh", "x", "c", "yl")
TAIL = 8
SWAP = [(0, 1), (1, 0)]
VMEM = pltpu.VMEM
SMALL = pltpu.CompilerParams(vmem_limit_bytes=4 * 2**20)
LARGE = pltpu.CompilerParams(vmem_limit_bytes=24 * 2**20)


def split3(v):
    hi = lax.reduce_precision(v, 8, 7)
    rest = v - hi
    mid = lax.reduce_precision(rest, 8, 7)
    return hi, mid, rest - mid


def spread(block, axes, n):
    copies = jnp.broadcast_to(block[None], (n,) + block.shape)
    return lax.all_to_all(copies, axes, 0, 0, tiled=True)


def block_shift(ref, z, sub):
    tail = ref[z, sub : sub + TAIL, :].astype(jnp.float32)
    return jnp.sum(tail, axis=0, keepdims=True)


def statistics_kernel(sub, own_ref, out_ref):
    nz = own_ref.shape[0]
    shifts = [block_shift(own_ref, z, sub) for z in range(nz)]
    top = functools.reduce(jnp.maximum, shifts)
    total = jnp.zeros_like(top)
    for z in range(nz):
        kern = own_ref[z, :sub, :].astype(jnp.float32)
        total += jnp.exp(shifts[z] - top) * jnp.sum(kern, axis=0, keepdims=True)
    log_sum = top + jnp.log(total)
    out_ref[...] = jnp.broadcast_to(log_sum[None], out_ref.shape)


def columns_kernel(sub, a, stats_ref, own_ref, b_ref, far_ref, col_ref, out_ref):
    nz = own_ref.shape[0]
    stats = stats_ref[:, 0, :]
    far = jnp.max(stats, axis=0, keepdims=True)
    col = b_ref[...] / jnp.sum(jnp.exp(stats - far), axis=0, keepdims=True)
    cols = jnp.zeros_like(col)
    for z in range(nz):
        factor = jnp.exp(block_shift(own_ref, z, sub) - far) * col
        plan = own_ref[z, :sub, :].astype(jnp.float32) * factor
        row = a / jnp.sum(plan, axis=1, keepdims=True)
        cols += jnp.sum(plan * row, axis=0, keepdims=True)
    far_ref[...] = far
    col_ref[...] = col
    out_ref[...] = jnp.broadcast_to(cols[None], out_ref.shape)


def mixture_kernel(
    sub,
    a,
    place_ref,
    sums_ref,
    far_ref,
    col_ref,
    b_ref,
    own_ref,
    other_ref,
    core_own_ref,
    core_other_ref,
    train_ref,
    core_train_ref,
    out_ref,
    plan_ref,
    cols_ref,
    train_vmem,
    sems,
):
    nz, _, nt = own_ref.shape
    half = nt // 2
    rows = nz * sub
    c, yl = place_ref[0], place_ref[1]
    copies = [
        pltpu.make_async_copy(src, train_vmem.at[k], sems.at[k])
        for k, src in enumerate((train_ref, core_train_ref))
    ]
    for copy in copies:
        copy.start()
    far = far_ref[...]
    total = jnp.sum(sums_ref[:, 0, :], axis=0, keepdims=True)
    col = col_ref[...] * (b_ref[...] / total)

    refs = ((own_ref, 0, 0), (other_ref, 0, 1), (core_own_ref, 1, 0), (core_other_ref, 1, 1))

    def step(z, cols):
        for ref, k, flip in refs:
            tail = ref[z, sub : sub + TAIL, :].astype(jnp.float32)
            shift = jnp.sum(tail, axis=0, keepdims=True)
            plan = ref[z, :sub, :].astype(jnp.float32) * (jnp.exp(shift - far) * col)
            plan = plan * (a / jnp.sum(plan, axis=1, keepdims=True))
            cols = cols + jnp.sum(plan, axis=0, keepdims=True)
            side = yl + flip * (1 - 2 * yl)
            start = pl.multiple_of(side * rows + z * sub, sub)
            small = plan.astype(jnp.bfloat16)
            plan_ref[0, k, pl.ds(start, sub), :] = small[:, :half]
            plan_ref[1, k, pl.ds(start, sub), :] = small[:, half:]
        return cols

    cols = lax.fori_loop(0, nz, step, jnp.zeros((1, nt), jnp.float32))
    cols_ref[0] = cols[:, :half]
    cols_ref[1] = cols[:, half:]

    mixed = jnp.zeros((half, train_ref.shape[1]), jnp.float32)
    for k in range(2):
        copies[k].wait()
        mixed += lax.dot_general(
            plan_ref[c, k],
            train_vmem[k],
            (((0,), (0,)), ((), ())),
            preferred_element_type=jnp.float32,
        )
    nchips, mine, _ = out_ref.shape
    feats = train_ref.shape[1]
    out_ref[:, :, :feats] = mixed.astype(jnp.bfloat16).reshape(nchips, mine, feats)

    my_cols = cols_ref[c]
    lane = lax.broadcasted_iota(jnp.int32, (128, 128), 1)
    per = 128 // mine
    for k in range(half // 128):
        v = jnp.broadcast_to(my_cols[:, k * 128 : (k + 1) * 128], (128, 128)).T
        hi = v.astype(jnp.bfloat16).astype(jnp.float32)
        mid = (v - hi).astype(jnp.bfloat16).astype(jnp.float32)
        lo = v - hi - mid
        tail = jnp.where(lane == 0, hi, jnp.where(lane == 1, mid, lo))
        out_ref[k * per : (k + 1) * per, :, feats:] = tail.astype(jnp.bfloat16).reshape(
            per, mine, 128
        )


def shards(train, target, mass):
    rows, feats = train.shape
    nc = lax.axis_size("c")
    nchips = lax.axis_size(CHIPS)
    nex = nc * nchips
    nz = lax.axis_size("z")
    nf = lax.axis_size(FEAT)
    nrows = lax.axis_size(ROWS)
    mine = target.shape[0]
    nt = mine * nex
    half = nt // nc
    sub = rows // nf
    scale = 3.0 / math.sqrt(F)
    a = 1.0 / (rows * nex)
    full = pl.BlockSpec(memory_space=VMEM)
    anywhere = pl.BlockSpec(memory_space=pl.ANY)

    core_train = lax.ppermute(train, "c", SWAP)

    same_core = spread(target, CHIPS, nchips).reshape(nchips * mine, feats)
    targets = spread(same_core, "c", nc).reshape(nt, feats)
    mass = mass.reshape(nchips, nc, mine).transpose(1, 0, 2).reshape(1, nt)
    b = mass / jnp.sum(mass)

    partial = lax.dot_general(
        train, targets, (((1,), (1,)), ((), ())), preferred_element_type=jnp.float32
    )
    parts = lax.all_to_all(partial.reshape(nf, sub, nt), PIECES, 0, 0, tiled=True)
    logits = jnp.sum(parts, axis=0) * scale

    top = jnp.max(logits, axis=1, keepdims=True)
    total = jnp.sum(jnp.exp(logits - top), axis=1, keepdims=True)
    v = logits - top - jnp.log(total)
    shift = jnp.max(v, axis=0)
    kern = jnp.exp(v - shift[None, :]).astype(jnp.bfloat16)
    tail = jnp.stack(split3(shift)).astype(jnp.bfloat16)
    tail = jnp.concatenate([tail, jnp.zeros((TAIL - 3, nt), jnp.bfloat16)], axis=0)
    block = jnp.concatenate([kern, tail], axis=0)

    own = spread(block, "z", nz).reshape(nz, sub + TAIL, nt)
    other = lax.ppermute(own, "yl", SWAP)
    core_own = lax.ppermute(own, "c", SWAP)

    vector = jax.ShapeDtypeStruct((1, nt), jnp.float32)
    copies = jax.ShapeDtypeStruct((nrows, 1, nt), jnp.float32)
    stats = pl.pallas_call(
        functools.partial(statistics_kernel, sub),
        out_shape=copies,
        in_specs=[full],
        out_specs=full,
        compiler_params=SMALL,
    )(own)
    stats = lax.all_to_all(stats, ROWS, 0, 0, tiled=True)
    far, col, sums = pl.pallas_call(
        functools.partial(columns_kernel, sub, a),
        out_shape=(vector, vector, copies),
        in_specs=[full] * 3,
        out_specs=(full,) * 3,
        compiler_params=SMALL,
    )(stats, own, b)
    sums = lax.all_to_all(sums, ROWS, 0, 0, tiled=True)
    other, _ = lax.optimization_barrier((other, col))
    core_other = lax.ppermute(other, "c", SWAP)

    place = jnp.stack([lax.axis_index("c"), lax.axis_index("yl")]).astype(jnp.int32)
    send = pl.pallas_call(
        functools.partial(mixture_kernel, sub, a),
        out_shape=jax.ShapeDtypeStruct((nchips, mine, feats + 128), jnp.bfloat16),
        in_specs=[pl.BlockSpec(memory_space=pltpu.SMEM)] + [full] * 8 + [anywhere] * 2,
        out_specs=full,
        scratch_shapes=[
            VMEM((nc, 2, rows, half), jnp.bfloat16),
            VMEM((nc, 1, half), jnp.float32),
            VMEM((2, rows, feats), jnp.bfloat16),
            pltpu.SemaphoreType.DMA((2,)),
        ],
        compiler_params=LARGE,
    )(place, sums, far, col, b, own, other, core_own, core_other, train, core_train)
    got = lax.all_to_all(send, CHIPS, 0, 0, tiled=True)
    got = jnp.sum(got.astype(jnp.float32), axis=0)
    mass_in = jnp.sum(got[:, feats : feats + 3], axis=1, keepdims=True)
    return (got[:, :feats] / mass_in).astype(jnp.bfloat16)


def solution(mesh):
    fine = Mesh(mesh.devices.reshape(4, 4, 2, 8, 2), ("yh", "x", "c", "z", "yl"))

    return jax.shard_map(
        shards,
        mesh=fine,
        in_specs=(P(EX, FEAT), P(EX, FEAT), P()),
        out_specs=P(EX, FEAT),
        check_vma=False,
    )
```

```python
import functools
import math

import jax
import jax.numpy as jnp
from jax import lax
from jax.experimental import pallas as pl
from jax.experimental.pallas import tpu as pltpu
from jax.sharding import Mesh, PartitionSpec as P


F = 16384
CHIPS = ("yh", "x")
EX = ("yh", "x", "c")
FEAT = ("z", "yl")
PIECES = ("yl", "z")
ROWS = ("yh", "x", "c", "yl")
TAIL = 8
SWAP = [(0, 1), (1, 0)]
VMEM = pltpu.VMEM
MIDDLE = pltpu.CompilerParams(vmem_limit_bytes=12 * 2**20)
SMALL = pltpu.CompilerParams(vmem_limit_bytes=4 * 2**20)
LARGE = pltpu.CompilerParams(vmem_limit_bytes=24 * 2**20)


SPAN = 249.0
BASE = 124.0


def round_up(v):
    return (v * (1.0 + 2.0**-7)).astype(jnp.bfloat16).astype(jnp.float32)


def encode_kernel(sub, train_ref, targets_ref, out_ref, partial_ref):
    _, _, nt = out_ref.shape
    rows = train_ref.shape[0]
    step = partial_ref.shape[0]
    on_diagonal = lax.broadcasted_iota(jnp.int32, (sub, 128), 0) == (
        lax.broadcasted_iota(jnp.int32, (sub, 128), 1)
    )
    for start in range(0, rows, step):
        partial_ref[...] = lax.dot_general(
            train_ref[start : start + step, :],
            targets_ref[...],
            (((1,), (1,)), ((), ())),
            preferred_element_type=jnp.float32,
        )
        for j in range(step // sub):
            k = start // sub + j
            p = partial_ref[j * sub : (j + 1) * sub, :]
            high = jnp.max(p, axis=1, keepdims=True)
            low = jnp.min(p, axis=1, keepdims=True)
            p = p - 0.5 * (high + low)
            wide = jnp.max(jnp.abs(p), axis=1, keepdims=True)
            row = round_up(jnp.maximum(wide, 1e-30))
            p = p * (1.0 / row)
            col = round_up(jnp.maximum(jnp.max(jnp.abs(p), axis=0, keepdims=True), 1e-30))
            u = p * (1.0 / col)
            code = jnp.exp2(jnp.minimum(jnp.abs(u), 1.0) * SPAN - BASE)
            out_ref[k, :sub, :] = jnp.where(u < 0, -code, code).astype(jnp.bfloat16)
            row = jnp.sum(jnp.where(on_diagonal, row, 0.0), axis=0, keepdims=True)
            row = jnp.concatenate([row, jnp.zeros((1, nt - 128), jnp.float32)], axis=1)
            index = lax.broadcasted_iota(jnp.int32, (TAIL, nt), 0)
            tail = jnp.where(index == 0, col, jnp.where(index == 1, row, 0.0))
            out_ref[k, sub : sub + TAIL, :] = tail.astype(jnp.bfloat16)


def rows_kernel(sub, scale, codes_ref, out_ref, logits_ref):
    nf, _, nt = codes_ref.shape
    nz = out_ref.shape[0]
    on_diagonal = lax.broadcasted_iota(jnp.int32, (sub, 128), 0) == (
        lax.broadcasted_iota(jnp.int32, (sub, 128), 1)
    )
    cols, rows = [], []
    for k in range(nf):
        tail = codes_ref[k, sub : sub + TAIL, :].astype(jnp.float32)
        cols.append(tail[0:1, :] * (scale / SPAN))
        row = jnp.where(on_diagonal, tail[1:2, :128], 0.0)
        rows.append(jnp.sum(row, axis=1, keepdims=True))
    for start in range(0, nt, 128):
        part = slice(start, start + 128)
        total = jnp.zeros((sub, 128), jnp.float32)
        for k in range(nf):
            code = codes_ref[k, :sub, part].astype(jnp.float32)
            size = jnp.log(jnp.abs(code)) * (1.0 / math.log(2.0)) + BASE
            size = jnp.where(code < 0, -size, size)
            total += size * cols[k][:, part] * rows[k]
        logits_ref[:, part] = total

    logits = logits_ref[...]
    top = jnp.max(logits, axis=1, keepdims=True)
    v = logits - top
    v = v - jnp.log(jnp.sum(jnp.exp(v), axis=1, keepdims=True))
    shift = jnp.max(v, axis=0, keepdims=True)
    kern = jnp.exp(v - shift).astype(jnp.bfloat16)
    hi = shift.astype(jnp.bfloat16).astype(jnp.float32)
    mid = (shift - hi).astype(jnp.bfloat16).astype(jnp.float32)
    index = lax.broadcasted_iota(jnp.int32, (TAIL, nt), 0)
    lo = jnp.where(index == 2, shift - hi - mid, 0.0)
    tail = jnp.where(index == 0, hi, jnp.where(index == 1, mid, lo)).astype(jnp.bfloat16)
    for z in range(nz):
        out_ref[z, :sub, :] = kern
        out_ref[z, sub : sub + TAIL, :] = tail


def spread(block, axes, n):
    copies = jnp.broadcast_to(block[None], (n,) + block.shape)
    return lax.all_to_all(copies, axes, 0, 0, tiled=True)


def block_shift(ref, z, sub):
    tail = ref[z, sub : sub + TAIL, :].astype(jnp.float32)
    return jnp.sum(tail, axis=0, keepdims=True)


def statistics_kernel(sub, own_ref, out_ref):
    nz = own_ref.shape[0]
    shifts = [block_shift(own_ref, z, sub) for z in range(nz)]
    top = functools.reduce(jnp.maximum, shifts)
    total = jnp.zeros_like(top)
    for z in range(nz):
        kern = own_ref[z, :sub, :].astype(jnp.float32)
        total += jnp.exp(shifts[z] - top) * jnp.sum(kern, axis=0, keepdims=True)
    log_sum = top + jnp.log(total)
    out_ref[...] = jnp.broadcast_to(log_sum[None], out_ref.shape)


def columns_kernel(sub, a, stats_ref, own_ref, b_ref, far_ref, col_ref, out_ref):
    nz = own_ref.shape[0]
    stats = stats_ref[:, 0, :]
    far = jnp.max(stats, axis=0, keepdims=True)
    col = b_ref[...] / jnp.sum(jnp.exp(stats - far), axis=0, keepdims=True)
    cols = jnp.zeros_like(col)
    for z in range(nz):
        factor = jnp.exp(block_shift(own_ref, z, sub) - far) * col
        plan = own_ref[z, :sub, :].astype(jnp.float32) * factor
        row = a / jnp.sum(plan, axis=1, keepdims=True)
        cols += jnp.sum(plan * row, axis=0, keepdims=True)
    far_ref[...] = far
    col_ref[...] = col
    out_ref[...] = jnp.broadcast_to(cols[None], out_ref.shape)


def mixture_kernel(
    sub,
    a,
    place_ref,
    sums_ref,
    far_ref,
    col_ref,
    b_ref,
    own_ref,
    other_ref,
    core_own_ref,
    core_other_ref,
    train_ref,
    core_train_ref,
    out_ref,
    plan_ref,
    cols_ref,
    train_vmem,
    sems,
):
    nz, _, nt = own_ref.shape
    half = nt // 2
    rows = nz * sub
    c, yl = place_ref[0], place_ref[1]
    copies = [
        pltpu.make_async_copy(src, train_vmem.at[k], sems.at[k])
        for k, src in enumerate((train_ref, core_train_ref))
    ]
    for copy in copies:
        copy.start()
    far = far_ref[...]
    total = jnp.sum(sums_ref[:, 0, :], axis=0, keepdims=True)
    col = col_ref[...] * (b_ref[...] / total)

    refs = ((own_ref, 0, 0), (other_ref, 0, 1), (core_own_ref, 1, 0), (core_other_ref, 1, 1))

    def step(z, cols):
        for ref, k, flip in refs:
            tail = ref[z, sub : sub + TAIL, :].astype(jnp.float32)
            shift = jnp.sum(tail, axis=0, keepdims=True)
            plan = ref[z, :sub, :].astype(jnp.float32) * (jnp.exp(shift - far) * col)
            plan = plan * (a / jnp.sum(plan, axis=1, keepdims=True))
            cols = cols + jnp.sum(plan, axis=0, keepdims=True)
            side = yl + flip * (1 - 2 * yl)
            start = pl.multiple_of(side * rows + z * sub, sub)
            small = plan.astype(jnp.bfloat16)
            plan_ref[0, k, pl.ds(start, sub), :] = small[:, :half]
            plan_ref[1, k, pl.ds(start, sub), :] = small[:, half:]
        return cols

    cols = lax.fori_loop(0, nz, step, jnp.zeros((1, nt), jnp.float32))
    cols_ref[0] = cols[:, :half]
    cols_ref[1] = cols[:, half:]

    mixed = jnp.zeros((half, train_ref.shape[1]), jnp.float32)
    for k in range(2):
        copies[k].wait()
        mixed += lax.dot_general(
            plan_ref[c, k],
            train_vmem[k],
            (((0,), (0,)), ((), ())),
            preferred_element_type=jnp.float32,
        )
    nchips, mine, _ = out_ref.shape
    feats = train_ref.shape[1]
    out_ref[:, :, :feats] = mixed.astype(jnp.bfloat16).reshape(nchips, mine, feats)

    my_cols = cols_ref[c]
    lane = lax.broadcasted_iota(jnp.int32, (128, 128), 1)
    per = 128 // mine
    for k in range(half // 128):
        v = jnp.broadcast_to(my_cols[:, k * 128 : (k + 1) * 128], (128, 128)).T
        hi = v.astype(jnp.bfloat16).astype(jnp.float32)
        mid = (v - hi).astype(jnp.bfloat16).astype(jnp.float32)
        lo = v - hi - mid
        tail = jnp.where(lane == 0, hi, jnp.where(lane == 1, mid, lo))
        out_ref[k * per : (k + 1) * per, :, feats:] = tail.astype(jnp.bfloat16).reshape(
            per, mine, 128
        )


def shards(train, target, mass):
    rows, feats = train.shape
    nc = lax.axis_size("c")
    nchips = lax.axis_size(CHIPS)
    nex = nc * nchips
    nz = lax.axis_size("z")
    nf = lax.axis_size(FEAT)
    nrows = lax.axis_size(ROWS)
    mine = target.shape[0]
    nt = mine * nex
    half = nt // nc
    sub = rows // nf
    scale = 3.0 / math.sqrt(F)
    a = 1.0 / (rows * nex)
    full = pl.BlockSpec(memory_space=VMEM)
    anywhere = pl.BlockSpec(memory_space=pl.ANY)

    core_train = lax.ppermute(train, "c", SWAP)

    same_core = spread(target, CHIPS, nchips).reshape(nchips * mine, feats)
    targets = spread(same_core, "c", nc).reshape(nt, feats)
    mass = mass.reshape(nchips, nc, mine).transpose(1, 0, 2).reshape(1, nt)
    b = mass / jnp.sum(mass)

    codes = pl.pallas_call(
        functools.partial(encode_kernel, sub),
        out_shape=jax.ShapeDtypeStruct((nf, sub + TAIL, nt), jnp.bfloat16),
        in_specs=[full] * 2,
        out_specs=full,
        scratch_shapes=[VMEM((4 * sub, nt), jnp.float32)],
        compiler_params=MIDDLE,
    )(train, targets)
    codes = lax.all_to_all(codes, PIECES, 0, 0, tiled=True)
    blocks = pl.pallas_call(
        functools.partial(rows_kernel, sub, scale),
        out_shape=jax.ShapeDtypeStruct((nz, sub + TAIL, nt), jnp.bfloat16),
        in_specs=[full],
        out_specs=full,
        scratch_shapes=[VMEM((sub, nt), jnp.float32)],
        compiler_params=MIDDLE,
    )(codes)

    own = lax.all_to_all(blocks, "z", 0, 0, tiled=True)
    other = lax.ppermute(own, "yl", SWAP)
    core_own = lax.ppermute(own, "c", SWAP)

    vector = jax.ShapeDtypeStruct((1, nt), jnp.float32)
    copies = jax.ShapeDtypeStruct((nrows, 1, nt), jnp.float32)
    stats = pl.pallas_call(
        functools.partial(statistics_kernel, sub),
        out_shape=copies,
        in_specs=[full],
        out_specs=full,
        compiler_params=SMALL,
    )(own)
    stats = lax.all_to_all(stats, ROWS, 0, 0, tiled=True)
    far, col, sums = pl.pallas_call(
        functools.partial(columns_kernel, sub, a),
        out_shape=(vector, vector, copies),
        in_specs=[full] * 3,
        out_specs=(full,) * 3,
        compiler_params=SMALL,
    )(stats, own, b)
    sums = lax.all_to_all(sums, ROWS, 0, 0, tiled=True)
    other, _ = lax.optimization_barrier((other, col))
    core_other = lax.ppermute(other, "c", SWAP)

    place = jnp.stack([lax.axis_index("c"), lax.axis_index("yl")]).astype(jnp.int32)
    send = pl.pallas_call(
        functools.partial(mixture_kernel, sub, a),
        out_shape=jax.ShapeDtypeStruct((nchips, mine, feats + 128), jnp.bfloat16),
        in_specs=[pl.BlockSpec(memory_space=pltpu.SMEM)] + [full] * 8 + [anywhere] * 2,
        out_specs=full,
        scratch_shapes=[
            VMEM((nc, 2, rows, half), jnp.bfloat16),
            VMEM((nc, 1, half), jnp.float32),
            VMEM((2, rows, feats), jnp.bfloat16),
            pltpu.SemaphoreType.DMA((2,)),
        ],
        compiler_params=LARGE,
    )(place, sums, far, col, b, own, other, core_own, core_other, train, core_train)
    got = lax.all_to_all(send, CHIPS, 0, 0, tiled=True)
    got = jnp.sum(got.astype(jnp.float32), axis=0)
    mass_in = jnp.sum(got[:, feats : feats + 3], axis=1, keepdims=True)
    return (got[:, :feats] / mass_in).astype(jnp.bfloat16)


def solution(mesh):
    fine = Mesh(mesh.devices.reshape(4, 4, 2, 8, 2), ("yh", "x", "c", "z", "yl"))

    return jax.shard_map(
        shards,
        mesh=fine,
        in_specs=(P(EX, FEAT), P(EX, FEAT), P()),
        out_specs=P(EX, FEAT),
        check_vma=False,
    )
```

```python
import functools
import math

import jax
import jax.numpy as jnp
from jax import lax
from jax.experimental import pallas as pl
from jax.experimental.pallas import tpu as pltpu
from jax.sharding import Mesh, PartitionSpec as P


F = 16384
CHIPS = ("yh", "x")
EX = ("yh", "x", "c")
FEAT = ("z", "yl")
PIECES = ("yl", "z")
ROWS = ("yh", "x", "c", "yl")
CHIP_ROWS = ("yh", "x", "yl")
LANES = 128
CODE_TAIL = 8
KERNEL_TAIL = 16
MIXTURE_TAIL = 8
SWAP = [(0, 1), (1, 0)]
VMEM = pltpu.VMEM
MIDDLE = pltpu.CompilerParams(vmem_limit_bytes=12 * 2**20)
SMALL = pltpu.CompilerParams(vmem_limit_bytes=4 * 2**20)
LARGE = pltpu.CompilerParams(vmem_limit_bytes=24 * 2**20)


SPAN = 249.0
BASE = 124.0


def round_up(v):
    return (v * (1.0 + 2.0**-7)).astype(jnp.bfloat16).astype(jnp.float32)


def split3(v):
    hi = v.astype(jnp.bfloat16).astype(jnp.float32)
    mid = (v - hi).astype(jnp.bfloat16).astype(jnp.float32)
    return hi, mid, v - hi - mid


def stack_rows(rows, height):
    index = lax.broadcasted_iota(jnp.int32, (height, LANES), 0)
    out = jnp.zeros((height, LANES), jnp.float32)
    for k, row in enumerate(rows):
        out = jnp.where(index == k, row, out)
    return out


def lane_blocks(v):
    return [v[:, k : k + LANES] for k in range(0, v.shape[1], LANES)]


def diagonal(sub):
    return lax.broadcasted_iota(jnp.int32, (sub, LANES), 0) == (
        lax.broadcasted_iota(jnp.int32, (sub, LANES), 1)
    )


def encode_kernel(sub, train_ref, targets_ref, out_ref, partial_ref):
    rows = train_ref.shape[0]
    step = partial_ref.shape[0]
    on_diagonal = diagonal(sub)
    for start in range(0, rows, step):
        partial_ref[...] = lax.dot_general(
            train_ref[start : start + step, :],
            targets_ref[...],
            (((1,), (1,)), ((), ())),
            preferred_element_type=jnp.float32,
        )
        for j in range(step // sub):
            k = start // sub + j
            p = partial_ref[j * sub : (j + 1) * sub, :]
            high = jnp.max(p, axis=1, keepdims=True)
            low = jnp.min(p, axis=1, keepdims=True)
            p = p - 0.5 * (high + low)
            wide = jnp.max(jnp.abs(p), axis=1, keepdims=True)
            row = round_up(jnp.maximum(wide, 1e-30))
            p = p * (1.0 / row)
            col = round_up(jnp.maximum(jnp.max(jnp.abs(p), axis=0, keepdims=True), 1e-30))
            u = p * (1.0 / col)
            code = jnp.exp2(jnp.minimum(jnp.abs(u), 1.0) * SPAN - BASE)
            code = jnp.where(u < 0, -code, code).astype(jnp.bfloat16)
            parts = lane_blocks(code)
            for n, part in enumerate(parts):
                out_ref[k, n * sub : (n + 1) * sub, :] = part
            row = jnp.sum(jnp.where(on_diagonal, row, 0.0), axis=0, keepdims=True)
            tail = stack_rows(lane_blocks(col) + [row], CODE_TAIL)
            out_ref[k, len(parts) * sub :, :] = tail.astype(jnp.bfloat16)


def rows_kernel(sub, scale, codes_ref, out_ref, logits_ref):
    nf = codes_ref.shape[0]
    nz = out_ref.shape[0]
    nl = logits_ref.shape[1] // LANES
    on_diagonal = diagonal(sub)
    tails, rows = [], []
    for k in range(nf):
        tail = codes_ref[k, nl * sub :, :].astype(jnp.float32)
        tails.append(tail * (scale / SPAN))
        row = jnp.where(on_diagonal, tail[nl : nl + 1, :], 0.0)
        rows.append(jnp.sum(row, axis=1, keepdims=True))
    for n in range(nl):
        total = jnp.zeros((sub, LANES), jnp.float32)
        for k in range(nf):
            code = codes_ref[k, n * sub : (n + 1) * sub, :].astype(jnp.float32)
            size = jnp.log(jnp.abs(code)) * (1.0 / math.log(2.0)) + BASE
            size = jnp.where(code < 0, -size, size)
            total += size * tails[k][n : n + 1, :] * rows[k]
        logits_ref[:, n * LANES : (n + 1) * LANES] = total

    logits = logits_ref[...]
    top = jnp.max(logits, axis=1, keepdims=True)
    v = logits - top
    v = v - jnp.log(jnp.sum(jnp.exp(v), axis=1, keepdims=True))
    shift = jnp.max(v, axis=0, keepdims=True)
    kern = lane_blocks(jnp.exp(v - shift).astype(jnp.bfloat16))
    terms = [row for term in split3(shift) for row in lane_blocks(term)]
    tail = stack_rows(terms, KERNEL_TAIL).astype(jnp.bfloat16)
    for z in range(nz):
        for n, part in enumerate(kern):
            out_ref[z, n * sub : (n + 1) * sub, :] = part
        out_ref[z, nl * sub :, :] = tail


def spread(block, axes, n):
    copies = jnp.broadcast_to(block[None], (n,) + block.shape)
    return lax.all_to_all(copies, axes, 0, 0, tiled=True)


def block_shift(ref, z, sub, nl):
    tail = ref[z, nl * sub :, :].astype(jnp.float32)
    return tail[:nl] + tail[nl : 2 * nl] + tail[2 * nl : 3 * nl]


def block_part(ref, z, sub, n):
    return ref[z, n * sub : (n + 1) * sub, :].astype(jnp.float32)


def statistics_kernel(sub, own_ref, out_ref):
    nz = own_ref.shape[0]
    nl = out_ref.shape[1]
    shifts = [block_shift(own_ref, z, sub, nl) for z in range(nz)]
    top = functools.reduce(jnp.maximum, shifts)
    total = [jnp.zeros((1, LANES), jnp.float32)] * nl
    for z in range(nz):
        factor = jnp.exp(shifts[z] - top)
        for n in range(nl):
            part = jnp.sum(block_part(own_ref, z, sub, n), axis=0, keepdims=True)
            total[n] = total[n] + factor[n : n + 1] * part
    log_sum = top + jnp.log(stack_rows(total, nl))
    out_ref[...] = jnp.broadcast_to(log_sum[None], out_ref.shape)


def columns_kernel(sub, a, stats_ref, own_ref, core_ref, b_ref, far_ref, col_ref, out_ref):
    nz = own_ref.shape[0]
    nl = out_ref.shape[1]
    stats = stats_ref[...]
    far = jnp.max(stats, axis=0)
    col = b_ref[...] / jnp.sum(jnp.exp(stats - far[None]), axis=0)
    cols = [jnp.zeros((1, LANES), jnp.float32)] * nl
    for z in range(nz):
        for ref in (own_ref, core_ref):
            factor = jnp.exp(block_shift(ref, z, sub, nl) - far) * col
            plan = [block_part(ref, z, sub, n) * factor[n : n + 1] for n in range(nl)]
            row = a / jnp.sum(functools.reduce(jnp.add, plan), axis=1, keepdims=True)
            for n in range(nl):
                cols[n] = cols[n] + jnp.sum(plan[n] * row, axis=0, keepdims=True)
    far_ref[...] = far
    col_ref[...] = col
    out_ref[...] = jnp.broadcast_to(stack_rows(cols, nl)[None], out_ref.shape)


def copy_kernel(in_ref, out_ref):
    out_ref[...] = in_ref[...]


def mixture_kernel(
    sub,
    a,
    place_ref,
    sums_ref,
    far_ref,
    col_ref,
    b_ref,
    own_ref,
    other_ref,
    core_own_ref,
    core_other_ref,
    train_ref,
    core_train_ref,
    out_ref,
    plan_ref,
    cols_ref,
    train_vmem,
    sems,
):
    nz = own_ref.shape[0]
    nl = sums_ref.shape[1]
    nh = nl // 2
    rows = nz * sub
    c, yl = place_ref[0], place_ref[1]
    copies = [
        pltpu.make_async_copy(src, train_vmem.at[k], sems.at[k])
        for k, src in enumerate((train_ref, core_train_ref))
    ]
    for copy in copies:
        copy.start()
    far = far_ref[...]
    col = col_ref[...] * (b_ref[...] / jnp.sum(sums_ref[...], axis=0))

    refs = ((own_ref, 0, 0), (other_ref, 0, 1), (core_own_ref, 1, 0), (core_other_ref, 1, 1))

    def step(z, cols):
        cols = list(cols)
        for ref, k, flip in refs:
            factor = jnp.exp(block_shift(ref, z, sub, nl) - far) * col
            plan = [block_part(ref, z, sub, n) * factor[n : n + 1] for n in range(nl)]
            row = a / jnp.sum(functools.reduce(jnp.add, plan), axis=1, keepdims=True)
            side = yl + flip * (1 - 2 * yl)
            start = pl.multiple_of(side * rows + z * sub, sub)
            for n in range(nl):
                part = plan[n] * row
                cols[n] = cols[n] + jnp.sum(part, axis=0, keepdims=True)
                lane = (n % nh) * LANES
                plan_ref[n // nh, k, pl.ds(start, sub), lane : lane + LANES] = part.astype(
                    jnp.bfloat16
                )
        return tuple(cols)

    cols = lax.fori_loop(0, nz, step, (jnp.zeros((1, LANES), jnp.float32),) * nl)
    for n in range(nl):
        cols_ref[n // nh, n % nh] = cols[n]

    half = nh * LANES
    mixed = jnp.zeros((half, train_ref.shape[1]), jnp.float32)
    for k in range(2):
        copies[k].wait()
        mixed += lax.dot_general(
            plan_ref[c, k],
            train_vmem[k],
            (((0,), (0,)), ((), ())),
            preferred_element_type=jnp.float32,
        )
    nchips = out_ref.shape[0]
    mine = half // nchips
    parts = lane_blocks(mixed.astype(jnp.bfloat16))
    for n, part in enumerate(parts):
        out_ref[:, n * mine : (n + 1) * mine, :] = part.reshape(nchips, mine, LANES)
    per = LANES // mine
    for n in range(nh):
        tail = stack_rows(split3(cols_ref[c, n]), MIXTURE_TAIL).astype(jnp.bfloat16)
        out_ref[n * per : (n + 1) * per, len(parts) * mine :, :] = jnp.broadcast_to(
            tail[None], (per, MIXTURE_TAIL, LANES)
        )


def output_kernel(place_ref, got_ref, out_ref):
    mine, feats = out_ref.shape
    nl = feats // LANES
    total = jnp.sum(got_ref[...].astype(jnp.float32), axis=0)
    mass = total[nl * mine : nl * mine + 1] + (
        total[nl * mine + 1 : nl * mine + 2] + total[nl * mine + 2 : nl * mine + 3]
    )
    lane = lax.broadcasted_iota(jnp.int32, (mine, LANES), 1)
    target = lax.broadcasted_iota(jnp.int32, (mine, LANES), 0) + place_ref[2] * mine
    mass = jnp.sum(jnp.where(lane == target, mass, 0.0), axis=1, keepdims=True)
    for n in range(nl):
        part = total[n * mine : (n + 1) * mine] / mass
        out_ref[:, n * LANES : (n + 1) * LANES] = part.astype(jnp.bfloat16)


def shards(train, target, mass):
    rows, feats = train.shape
    nc = lax.axis_size("c")
    nchips = lax.axis_size(CHIPS)
    nex = nc * nchips
    nz = lax.axis_size("z")
    nf = lax.axis_size(FEAT)
    mine = target.shape[0]
    nt = mine * nex
    nl = nt // LANES
    half = nt // nc
    sub = rows // nf
    scale = 3.0 / math.sqrt(F)
    a = 1.0 / (rows * nex)
    full = pl.BlockSpec(memory_space=VMEM)
    anywhere = pl.BlockSpec(memory_space=pl.ANY)
    scalars = pl.BlockSpec(memory_space=pltpu.SMEM)

    core_train = lax.ppermute(train, "c", SWAP)

    same_core = spread(target, CHIPS, nchips).reshape(nchips * mine, feats)
    targets = spread(same_core, "c", nc).reshape(nt, feats)
    mass = mass.reshape(nchips, nc, mine).transpose(1, 0, 2).reshape(nl, LANES)
    b = mass / jnp.sum(mass)

    codes = pl.pallas_call(
        functools.partial(encode_kernel, sub),
        out_shape=jax.ShapeDtypeStruct((nf, nl * sub + CODE_TAIL, LANES), jnp.bfloat16),
        in_specs=[full] * 2,
        out_specs=full,
        scratch_shapes=[VMEM((4 * sub, nt), jnp.float32)],
        compiler_params=MIDDLE,
    )(train, targets)
    codes = lax.all_to_all(codes, PIECES, 0, 0, tiled=True)
    blocks = pl.pallas_call(
        functools.partial(rows_kernel, sub, scale),
        out_shape=jax.ShapeDtypeStruct((nz, nl * sub + KERNEL_TAIL, LANES), jnp.bfloat16),
        in_specs=[full],
        out_specs=full,
        scratch_shapes=[VMEM((sub, nt), jnp.float32)],
        compiler_params=MIDDLE,
    )(codes)

    own = lax.all_to_all(blocks, "z", 0, 0, tiled=True)
    other = lax.ppermute(own, "yl", SWAP)
    core_own = lax.ppermute(own, "c", SWAP)

    def copies(axes):
        return jax.ShapeDtypeStruct((lax.axis_size(axes), nl, LANES), jnp.float32)

    vector = jax.ShapeDtypeStruct((nl, LANES), jnp.float32)
    stats = pl.pallas_call(
        functools.partial(statistics_kernel, sub),
        out_shape=copies(ROWS),
        in_specs=[full],
        out_specs=full,
        compiler_params=SMALL,
    )(own)
    stats = lax.all_to_all(stats, ROWS, 0, 0, tiled=True)
    far, col, sums = pl.pallas_call(
        functools.partial(columns_kernel, sub, a),
        out_shape=(vector, vector, copies(CHIP_ROWS)),
        in_specs=[full] * 4,
        out_specs=(full,) * 3,
        compiler_params=SMALL,
    )(stats, own, core_own, b)
    sums = lax.all_to_all(sums, CHIP_ROWS, 0, 0, tiled=True)
    other_copy = pl.pallas_call(
        copy_kernel,
        out_shape=jax.ShapeDtypeStruct(other.shape, other.dtype),
        in_specs=[full],
        out_specs=full,
        compiler_params=SMALL,
    )(other)
    core_other = lax.ppermute(other_copy, "c", SWAP)

    slot = jnp.bitwise_and(lax.axis_index(CHIPS), LANES // mine - 1)
    place = jnp.stack([lax.axis_index("c"), lax.axis_index("yl"), slot]).astype(jnp.int32)
    block = feats // LANES * mine + MIXTURE_TAIL
    send = pl.pallas_call(
        functools.partial(mixture_kernel, sub, a),
        out_shape=jax.ShapeDtypeStruct((nchips, block, LANES), jnp.bfloat16),
        in_specs=[scalars] + [full] * 8 + [anywhere] * 2,
        out_specs=full,
        scratch_shapes=[
            VMEM((nc, 2, rows, half), jnp.bfloat16),
            VMEM((nc, nl // nc, 1, LANES), jnp.float32),
            VMEM((2, rows, feats), jnp.bfloat16),
            pltpu.SemaphoreType.DMA((2,)),
        ],
        compiler_params=LARGE,
    )(place, sums, far, col, b, own, other, core_own, core_other, train, core_train)
    got = lax.all_to_all(send, CHIPS, 0, 0, tiled=True)
    return pl.pallas_call(
        output_kernel,
        out_shape=jax.ShapeDtypeStruct((mine, feats), jnp.bfloat16),
        in_specs=[scalars, full],
        out_specs=full,
        compiler_params=SMALL,
    )(place, got)


def solution(mesh):
    fine = Mesh(mesh.devices.reshape(4, 4, 2, 8, 2), ("yh", "x", "c", "z", "yl"))

    return jax.shard_map(
        shards,
        mesh=fine,
        in_specs=(P(EX, FEAT), P(EX, FEAT), P()),
        out_specs=P(EX, FEAT),
        check_vma=False,
    )
```

```python
import functools
import math

import jax
import jax.numpy as jnp
from jax import lax
from jax.experimental import pallas as pl
from jax.experimental.pallas import tpu as pltpu
from jax.sharding import Mesh, PartitionSpec as P


F = 16384
CHIPS = ("yh", "x")
EX = ("yh", "x", "c")
FEAT = ("z", "yl")
PIECES = ("yl", "z")
ROWS = ("yh", "x", "c", "yl")
CHIP_ROWS = ("yh", "x", "yl")
LANES = 128
CODE_TAIL = 8
KERNEL_TAIL = 16
MIXTURE_TAIL = 8
SWAP = [(0, 1), (1, 0)]
VMEM = pltpu.VMEM
MIDDLE = pltpu.CompilerParams(vmem_limit_bytes=12 * 2**20)
SMALL = pltpu.CompilerParams(vmem_limit_bytes=4 * 2**20)
LARGE = pltpu.CompilerParams(vmem_limit_bytes=24 * 2**20)


SPAN = 249.0
BASE = 124.0


def round_up(v):
    return (v * (1.0 + 2.0**-7)).astype(jnp.bfloat16).astype(jnp.float32)


def split3(v):
    hi = v.astype(jnp.bfloat16).astype(jnp.float32)
    mid = (v - hi).astype(jnp.bfloat16).astype(jnp.float32)
    return hi, mid, v - hi - mid


def stack_rows(rows, height):
    index = lax.broadcasted_iota(jnp.int32, (height, LANES), 0)
    out = jnp.zeros((height, LANES), jnp.float32)
    for k, row in enumerate(rows):
        out = jnp.where(index == k, row, out)
    return out


def lane_blocks(v):
    return [v[:, k : k + LANES] for k in range(0, v.shape[1], LANES)]


def diagonal(sub):
    return lax.broadcasted_iota(jnp.int32, (sub, LANES), 0) == (
        lax.broadcasted_iota(jnp.int32, (sub, LANES), 1)
    )


def encode_kernel(sub, train_ref, targets_ref, out_ref, partial_ref):
    rows = train_ref.shape[0]
    step = partial_ref.shape[0]
    on_diagonal = diagonal(sub)
    for start in range(0, rows, step):
        partial_ref[...] = lax.dot_general(
            train_ref[start : start + step, :],
            targets_ref[...],
            (((1,), (1,)), ((), ())),
            preferred_element_type=jnp.float32,
        )
        for j in range(step // sub):
            k = start // sub + j
            p = partial_ref[j * sub : (j + 1) * sub, :]
            high = jnp.max(p, axis=1, keepdims=True)
            low = jnp.min(p, axis=1, keepdims=True)
            p = p - 0.5 * (high + low)
            wide = jnp.max(jnp.abs(p), axis=1, keepdims=True)
            row = round_up(jnp.maximum(wide, 1e-30))
            p = p * (1.0 / row)
            col = round_up(jnp.maximum(jnp.max(jnp.abs(p), axis=0, keepdims=True), 1e-30))
            u = p * (1.0 / col)
            code = jnp.exp2(jnp.minimum(jnp.abs(u), 1.0) * SPAN - BASE)
            code = jnp.where(u < 0, -code, code).astype(jnp.bfloat16)
            parts = lane_blocks(code)
            for n, part in enumerate(parts):
                out_ref[k, n * sub : (n + 1) * sub, :] = part
            row = jnp.sum(jnp.where(on_diagonal, row, 0.0), axis=0, keepdims=True)
            tail = stack_rows(lane_blocks(col) + [row], CODE_TAIL)
            out_ref[k, len(parts) * sub :, :] = tail.astype(jnp.bfloat16)


def rows_kernel(sub, scale, codes_ref, out_ref, logits_ref):
    nf = codes_ref.shape[0]
    nz = out_ref.shape[0]
    nl = logits_ref.shape[1] // LANES
    on_diagonal = diagonal(sub)
    tails, rows = [], []
    for k in range(nf):
        tail = codes_ref[k, nl * sub :, :].astype(jnp.float32)
        tails.append(tail * (scale / SPAN))
        row = jnp.where(on_diagonal, tail[nl : nl + 1, :], 0.0)
        rows.append(jnp.sum(row, axis=1, keepdims=True))
    for n in range(nl):
        total = jnp.zeros((sub, LANES), jnp.float32)
        for k in range(nf):
            code = codes_ref[k, n * sub : (n + 1) * sub, :].astype(jnp.float32)
            size = jnp.log(jnp.abs(code)) * (1.0 / math.log(2.0)) + BASE
            size = jnp.where(code < 0, -size, size)
            total += size * tails[k][n : n + 1, :] * rows[k]
        logits_ref[:, n * LANES : (n + 1) * LANES] = total

    logits = logits_ref[...]
    top = jnp.max(logits, axis=1, keepdims=True)
    v = logits - top
    v = v - jnp.log(jnp.sum(jnp.exp(v), axis=1, keepdims=True))
    shift = jnp.max(v, axis=0, keepdims=True)
    kern = lane_blocks(jnp.exp(v - shift).astype(jnp.bfloat16))
    terms = [row for term in split3(shift) for row in lane_blocks(term)]
    tail = stack_rows(terms, KERNEL_TAIL).astype(jnp.bfloat16)
    for z in range(nz):
        for n, part in enumerate(kern):
            out_ref[z, n * sub : (n + 1) * sub, :] = part
        out_ref[z, nl * sub :, :] = tail


def spread(block, axes, n):
    copies = jnp.broadcast_to(block[None], (n,) + block.shape)
    return lax.all_to_all(copies, axes, 0, 0, tiled=True)


def block_shift(ref, z, sub, nl):
    tail = ref[z, nl * sub :, :].astype(jnp.float32)
    return tail[:nl] + tail[nl : 2 * nl] + tail[2 * nl : 3 * nl]


def block_part(ref, z, sub, n):
    return ref[z, n * sub : (n + 1) * sub, :].astype(jnp.float32)


def statistics_kernel(sub, own_ref, out_ref):
    nz = own_ref.shape[0]
    nl = out_ref.shape[1]
    shifts = [block_shift(own_ref, z, sub, nl) for z in range(nz)]
    top = functools.reduce(jnp.maximum, shifts)
    total = [jnp.zeros((1, LANES), jnp.float32)] * nl
    for z in range(nz):
        factor = jnp.exp(shifts[z] - top)
        for n in range(nl):
            part = jnp.sum(block_part(own_ref, z, sub, n), axis=0, keepdims=True)
            total[n] = total[n] + factor[n : n + 1] * part
    log_sum = top + jnp.log(stack_rows(total, nl))
    out_ref[...] = jnp.broadcast_to(log_sum[None], out_ref.shape)


def columns_kernel(sub, a, stats_ref, own_ref, core_ref, b_ref, far_ref, col_ref, out_ref):
    nz = own_ref.shape[0]
    nl = out_ref.shape[1]
    stats = stats_ref[...]
    far = jnp.max(stats, axis=0)
    col = b_ref[...] / jnp.sum(jnp.exp(stats - far[None]), axis=0)
    cols = [jnp.zeros((1, LANES), jnp.float32)] * nl
    for z in range(nz):
        for ref in (own_ref, core_ref):
            factor = jnp.exp(block_shift(ref, z, sub, nl) - far) * col
            plan = [block_part(ref, z, sub, n) * factor[n : n + 1] for n in range(nl)]
            row = a / jnp.sum(functools.reduce(jnp.add, plan), axis=1, keepdims=True)
            for n in range(nl):
                cols[n] = cols[n] + jnp.sum(plan[n] * row, axis=0, keepdims=True)
    far_ref[...] = far
    col_ref[...] = col
    out_ref[...] = jnp.broadcast_to(stack_rows(cols, nl)[None], out_ref.shape)


def copy_kernel(in_ref, out_ref):
    out_ref[...] = in_ref[...]


def mixture_kernel(
    sub,
    a,
    place_ref,
    sums_ref,
    far_ref,
    col_ref,
    b_ref,
    own_ref,
    other_ref,
    core_own_ref,
    core_other_ref,
    train_ref,
    core_train_ref,
    out_ref,
    plan_ref,
    cols_ref,
    blocks_vmem,
    train_vmem,
    sems,
):
    _, nz, _, _ = blocks_vmem.shape
    nl = sums_ref.shape[1]
    nh = nl // 2
    rows = nz * sub
    c, yl = place_ref[0], place_ref[1]
    sources = (own_ref, core_own_ref, other_ref, core_other_ref)
    loads = [
        pltpu.make_async_copy(src, blocks_vmem.at[k], sems.at[k])
        for k, src in enumerate(sources)
    ]
    copies = [
        pltpu.make_async_copy(src, train_vmem.at[k], sems.at[len(sources) + k])
        for k, src in enumerate((train_ref, core_train_ref))
    ]
    for copy in loads + copies:
        copy.start()
    far = far_ref[...]
    col = col_ref[...] * (b_ref[...] / jnp.sum(sums_ref[...], axis=0))

    def step(i, z, cols):
        cols = list(cols)
        ref = blocks_vmem.at[i]
        factor = jnp.exp(block_shift(ref, z, sub, nl) - far) * col
        plan = [block_part(ref, z, sub, n) * factor[n : n + 1] for n in range(nl)]
        row = a / jnp.sum(functools.reduce(jnp.add, plan), axis=1, keepdims=True)
        side = yl if i < 2 else 1 - yl
        start = pl.multiple_of(side * rows + z * sub, sub)
        for n in range(nl):
            part = plan[n] * row
            cols[n] = cols[n] + jnp.sum(part, axis=0, keepdims=True)
            lane = (n % nh) * LANES
            plan_ref[n // nh, i % 2, pl.ds(start, sub), lane : lane + LANES] = part.astype(
                jnp.bfloat16
            )
        return tuple(cols)

    cols = (jnp.zeros((1, LANES), jnp.float32),) * nl
    for i in range(len(sources)):
        loads[i].wait()
        cols = lax.fori_loop(0, nz, functools.partial(step, i), cols, unroll=2)
    for n in range(nl):
        cols_ref[n // nh, n % nh] = cols[n]

    half = nh * LANES
    mixed = jnp.zeros((half, train_ref.shape[1]), jnp.float32)
    for k in range(2):
        copies[k].wait()
        mixed += lax.dot_general(
            plan_ref[c, k],
            train_vmem[k],
            (((0,), (0,)), ((), ())),
            preferred_element_type=jnp.float32,
        )
    nchips = out_ref.shape[0]
    mine = half // nchips
    parts = lane_blocks(mixed.astype(jnp.bfloat16))
    for n, part in enumerate(parts):
        out_ref[:, n * mine : (n + 1) * mine, :] = part.reshape(nchips, mine, LANES)
    per = LANES // mine
    for n in range(nh):
        tail = stack_rows(split3(cols_ref[c, n]), MIXTURE_TAIL).astype(jnp.bfloat16)
        out_ref[n * per : (n + 1) * per, len(parts) * mine :, :] = jnp.broadcast_to(
            tail[None], (per, MIXTURE_TAIL, LANES)
        )


def output_kernel(place_ref, got_ref, out_ref):
    mine, feats = out_ref.shape
    nl = feats // LANES
    total = jnp.sum(got_ref[...].astype(jnp.float32), axis=0)
    mass = total[nl * mine : nl * mine + 1] + (
        total[nl * mine + 1 : nl * mine + 2] + total[nl * mine + 2 : nl * mine + 3]
    )
    lane = lax.broadcasted_iota(jnp.int32, (mine, LANES), 1)
    target = lax.broadcasted_iota(jnp.int32, (mine, LANES), 0) + place_ref[2] * mine
    mass = jnp.sum(jnp.where(lane == target, mass, 0.0), axis=1, keepdims=True)
    for n in range(nl):
        part = total[n * mine : (n + 1) * mine] / mass
        out_ref[:, n * LANES : (n + 1) * LANES] = part.astype(jnp.bfloat16)


def shards(train, target, mass):
    rows, feats = train.shape
    nc = lax.axis_size("c")
    nchips = lax.axis_size(CHIPS)
    nex = nc * nchips
    nz = lax.axis_size("z")
    nf = lax.axis_size(FEAT)
    mine = target.shape[0]
    nt = mine * nex
    nl = nt // LANES
    half = nt // nc
    sub = rows // nf
    scale = 3.0 / math.sqrt(F)
    a = 1.0 / (rows * nex)
    full = pl.BlockSpec(memory_space=VMEM)
    anywhere = pl.BlockSpec(memory_space=pl.ANY)
    scalars = pl.BlockSpec(memory_space=pltpu.SMEM)

    core_train = lax.ppermute(train, "c", SWAP)

    same_core = spread(target, CHIPS, nchips).reshape(nchips * mine, feats)
    mass = mass.reshape(nchips, nc, mine).transpose(1, 0, 2).reshape(nl, LANES)
    b = mass / jnp.sum(mass)
    same_core, b = lax.optimization_barrier((same_core, b))
    targets = spread(same_core, "c", nc).reshape(nt, feats)

    codes = pl.pallas_call(
        functools.partial(encode_kernel, sub),
        out_shape=jax.ShapeDtypeStruct((nf, nl * sub + CODE_TAIL, LANES), jnp.bfloat16),
        in_specs=[full] * 2,
        out_specs=full,
        scratch_shapes=[VMEM((4 * sub, nt), jnp.float32)],
        compiler_params=MIDDLE,
    )(train, targets)
    codes = lax.all_to_all(codes, PIECES, 0, 0, tiled=True)
    blocks = pl.pallas_call(
        functools.partial(rows_kernel, sub, scale),
        out_shape=jax.ShapeDtypeStruct((nz, nl * sub + KERNEL_TAIL, LANES), jnp.bfloat16),
        in_specs=[full],
        out_specs=full,
        scratch_shapes=[VMEM((sub, nt), jnp.float32)],
        compiler_params=MIDDLE,
    )(codes)

    own = lax.all_to_all(blocks, "z", 0, 0, tiled=True)
    other = lax.ppermute(own, "yl", SWAP)
    core_own = lax.ppermute(own, "c", SWAP)

    def copies(axes):
        return jax.ShapeDtypeStruct((lax.axis_size(axes), nl, LANES), jnp.float32)

    vector = jax.ShapeDtypeStruct((nl, LANES), jnp.float32)
    stats = pl.pallas_call(
        functools.partial(statistics_kernel, sub),
        out_shape=copies(ROWS),
        in_specs=[full],
        out_specs=full,
        compiler_params=SMALL,
    )(own)
    stats = lax.all_to_all(stats, ROWS, 0, 0, tiled=True)
    far, col, sums = pl.pallas_call(
        functools.partial(columns_kernel, sub, a),
        out_shape=(vector, vector, copies(CHIP_ROWS)),
        in_specs=[full] * 4,
        out_specs=(full,) * 3,
        compiler_params=SMALL,
    )(stats, own, core_own, b)
    sums = lax.all_to_all(sums, CHIP_ROWS, 0, 0, tiled=True)
    other_copy = pl.pallas_call(
        copy_kernel,
        out_shape=jax.ShapeDtypeStruct(other.shape, other.dtype),
        in_specs=[full],
        out_specs=full,
        compiler_params=SMALL,
    )(other)
    core_other = lax.ppermute(other_copy, "c", SWAP)

    slot = jnp.bitwise_and(lax.axis_index(CHIPS), LANES // mine - 1)
    place = jnp.stack([lax.axis_index("c"), lax.axis_index("yl"), slot]).astype(jnp.int32)
    block = feats // LANES * mine + MIXTURE_TAIL
    send = pl.pallas_call(
        functools.partial(mixture_kernel, sub, a),
        out_shape=jax.ShapeDtypeStruct((nchips, block, LANES), jnp.bfloat16),
        in_specs=[scalars] + [full] * 4 + [anywhere] * 6,
        out_specs=full,
        scratch_shapes=[
            VMEM((nc, 2, rows, half), jnp.bfloat16),
            VMEM((nc, nl // nc, 1, LANES), jnp.float32),
            VMEM((4,) + own.shape, jnp.bfloat16),
            VMEM((2, rows, feats), jnp.bfloat16),
            pltpu.SemaphoreType.DMA((6,)),
        ],
        compiler_params=LARGE,
    )(place, sums, far, col, b, own, other, core_own, core_other, train, core_train)
    got = lax.all_to_all(send, CHIPS, 0, 0, tiled=True)
    return pl.pallas_call(
        output_kernel,
        out_shape=jax.ShapeDtypeStruct((mine, feats), jnp.bfloat16),
        in_specs=[scalars, full],
        out_specs=full,
        compiler_params=SMALL,
    )(place, got)


def solution(mesh):
    fine = Mesh(mesh.devices.reshape(4, 4, 2, 8, 2), ("yh", "x", "c", "z", "yl"))

    return jax.shard_map(
        shards,
        mesh=fine,
        in_specs=(P(EX, FEAT), P(EX, FEAT), P()),
        out_specs=P(EX, FEAT),
        check_vma=False,
    )
```

```python
import functools
import math

import jax
import jax.numpy as jnp
from jax import lax
from jax.experimental import pallas as pl
from jax.experimental.pallas import tpu as pltpu
from jax.sharding import Mesh, PartitionSpec as P


F = 16384
CHIPS = ("yh", "x")
EX = ("yh", "x", "c")
FEAT = ("z", "yl")
PIECES = ("yl", "z")
ROWS = ("yh", "x", "c", "yl")
CHIP_ROWS = ("yh", "x", "yl")
LANES = 128
CODE_TAIL = 8
KERNEL_TAIL = 16
MIXTURE_TAIL = 8
SWAP = [(0, 1), (1, 0)]
VMEM = pltpu.VMEM
MIDDLE = pltpu.CompilerParams(vmem_limit_bytes=12 * 2**20)
SMALL = pltpu.CompilerParams(vmem_limit_bytes=4 * 2**20)
LARGE = pltpu.CompilerParams(vmem_limit_bytes=24 * 2**20)


SPAN = 249.0
BASE = 124.0


def round_up(v):
    return (v * (1.0 + 2.0**-7)).astype(jnp.bfloat16).astype(jnp.float32)


def split3(v):
    hi = v.astype(jnp.bfloat16).astype(jnp.float32)
    mid = (v - hi).astype(jnp.bfloat16).astype(jnp.float32)
    return hi, mid, v - hi - mid


def stack_rows(rows, height):
    index = lax.broadcasted_iota(jnp.int32, (height, LANES), 0)
    out = jnp.zeros((height, LANES), jnp.float32)
    for k, row in enumerate(rows):
        out = jnp.where(index == k, row, out)
    return out


def lane_blocks(v):
    return [v[:, k : k + LANES] for k in range(0, v.shape[1], LANES)]


def diagonal(sub):
    return lax.broadcasted_iota(jnp.int32, (sub, LANES), 0) == (
        lax.broadcasted_iota(jnp.int32, (sub, LANES), 1)
    )


def encode_kernel(sub, train_ref, targets_ref, out_ref, partial_ref):
    rows = train_ref.shape[0]
    step = partial_ref.shape[1]
    on_diagonal = diagonal(sub)
    for start in range(0, rows, step):
        slot = start // step % 2
        partial_ref[slot] = lax.dot_general(
            train_ref[start : start + step, :],
            targets_ref[...],
            (((1,), (1,)), ((), ())),
            preferred_element_type=jnp.float32,
        )
        for j in range(step // sub):
            k = start // sub + j
            p = partial_ref[slot, j * sub : (j + 1) * sub, :]
            high = jnp.max(p, axis=1, keepdims=True)
            low = jnp.min(p, axis=1, keepdims=True)
            p = p - 0.5 * (high + low)
            wide = jnp.max(jnp.abs(p), axis=1, keepdims=True)
            row = round_up(jnp.maximum(wide, 1e-30))
            p = p * (1.0 / row)
            col = round_up(jnp.maximum(jnp.max(jnp.abs(p), axis=0, keepdims=True), 1e-30))
            u = p * (1.0 / col)
            code = jnp.exp2(jnp.abs(u) * SPAN - BASE)
            code = jnp.where(u < 0, -code, code).astype(jnp.bfloat16)
            parts = lane_blocks(code)
            for n, part in enumerate(parts):
                out_ref[k, n * sub : (n + 1) * sub, :] = part
            row = jnp.sum(jnp.where(on_diagonal, row, 0.0), axis=0, keepdims=True)
            tail = stack_rows(lane_blocks(col) + [row], CODE_TAIL)
            out_ref[k, len(parts) * sub :, :] = tail.astype(jnp.bfloat16)


def rows_kernel(sub, scale, codes_ref, out_ref, logits_ref):
    nf = codes_ref.shape[0]
    nz = out_ref.shape[0]
    nl = logits_ref.shape[1] // LANES
    on_diagonal = diagonal(sub)
    tails, rows = [], []
    for k in range(nf):
        tail = codes_ref[k, nl * sub :, :].astype(jnp.float32)
        tails.append(tail * (scale / SPAN))
        row = jnp.where(on_diagonal, tail[nl : nl + 1, :], 0.0)
        rows.append(jnp.sum(row, axis=1, keepdims=True))
    for n in range(nl):
        total = jnp.zeros((sub, LANES), jnp.float32)
        for k in range(nf):
            code = codes_ref[k, n * sub : (n + 1) * sub, :].astype(jnp.float32)
            size = jnp.log(jnp.abs(code)) * (1.0 / math.log(2.0)) + BASE
            size = jnp.where(code < 0, -size, size)
            total += size * tails[k][n : n + 1, :] * rows[k]
        logits_ref[:, n * LANES : (n + 1) * LANES] = total

    logits = logits_ref[...]
    top = jnp.max(logits, axis=1, keepdims=True)
    v = logits - top
    v = v - jnp.log(jnp.sum(jnp.exp(v), axis=1, keepdims=True))
    shift = jnp.max(v, axis=0, keepdims=True)
    kern = lane_blocks(jnp.exp(v - shift).astype(jnp.bfloat16))
    terms = [row for term in split3(shift) for row in lane_blocks(term)]
    tail = stack_rows(terms, KERNEL_TAIL).astype(jnp.bfloat16)
    for z in range(nz):
        for n, part in enumerate(kern):
            out_ref[z, n * sub : (n + 1) * sub, :] = part
        out_ref[z, nl * sub :, :] = tail


def spread(block, axes, n):
    copies = jnp.broadcast_to(block[None], (n,) + block.shape)
    return lax.all_to_all(copies, axes, 0, 0, tiled=True)


def block_shift(ref, z, sub, nl):
    tail = ref[z, nl * sub :, :].astype(jnp.float32)
    return tail[:nl] + tail[nl : 2 * nl] + tail[2 * nl : 3 * nl]


def block_part(ref, z, sub, n):
    return ref[z, n * sub : (n + 1) * sub, :].astype(jnp.float32)


def group_sum(v):
    return functools.reduce(jnp.add, [v[k : k + 8] for k in range(0, v.shape[0], 8)])


def statistics_kernel(sub, own_ref, out_ref):
    nz = own_ref.shape[0]
    nl = out_ref.shape[1]
    shifts = [block_shift(own_ref, z, sub, nl) for z in range(nz)]
    top = functools.reduce(jnp.maximum, shifts)
    total = [jnp.zeros((8, LANES), jnp.float32)] * nl
    for z in range(nz):
        factor = jnp.exp(shifts[z] - top)
        for n in range(nl):
            part = group_sum(block_part(own_ref, z, sub, n))
            total[n] = total[n] + factor[n : n + 1] * part
    total = [jnp.sum(t, axis=0, keepdims=True) for t in total]
    log_sum = top + jnp.log(stack_rows(total, nl))
    out_ref[...] = jnp.broadcast_to(log_sum[None], out_ref.shape)


def columns_kernel(sub, a, stats_ref, own_ref, core_ref, mass_ref, far_ref, col_ref, b_ref, out_ref):
    nz = own_ref.shape[0]
    nl = out_ref.shape[1]
    stats = stats_ref[...]
    far = jnp.max(stats, axis=0)
    b = mass_ref[...] / jnp.sum(mass_ref[...])
    col = b / jnp.sum(jnp.exp(stats - far[None]), axis=0)
    cols = [jnp.zeros((8, LANES), jnp.float32)] * nl
    for z in range(nz):
        for ref in (own_ref, core_ref):
            factor = jnp.exp(block_shift(ref, z, sub, nl) - far) * col
            plan = [block_part(ref, z, sub, n) * factor[n : n + 1] for n in range(nl)]
            row = a / jnp.sum(functools.reduce(jnp.add, plan), axis=1, keepdims=True)
            for n in range(nl):
                cols[n] = cols[n] + group_sum(plan[n] * row)
    cols = [jnp.sum(t, axis=0, keepdims=True) for t in cols]
    far_ref[...] = far
    b_ref[...] = b
    col_ref[...] = col
    out_ref[...] = jnp.broadcast_to(stack_rows(cols, nl)[None], out_ref.shape)


def copy_kernel(in_ref, out_ref):
    out_ref[...] = in_ref[...]


def mixture_kernel(
    sub,
    a,
    place_ref,
    sums_ref,
    far_ref,
    col_ref,
    b_ref,
    own_ref,
    other_ref,
    core_own_ref,
    core_other_ref,
    train_ref,
    core_train_ref,
    out_ref,
    plan_ref,
    blocks_vmem,
    train_vmem,
    sems,
):
    _, nz, _, _ = blocks_vmem.shape
    nl = sums_ref.shape[1]
    nh = nl // 2
    rows = nz * sub
    c, yl = place_ref[0], place_ref[1]
    sources = (own_ref, core_own_ref, other_ref, core_other_ref)
    loads = [
        pltpu.make_async_copy(src, blocks_vmem.at[k], sems.at[k])
        for k, src in enumerate(sources)
    ]
    copies = [
        pltpu.make_async_copy(src, train_vmem.at[k], sems.at[len(sources) + k])
        for k, src in enumerate((train_ref, core_train_ref))
    ]
    for copy in loads + copies:
        copy.start()
    far = far_ref[...]
    col = col_ref[...] * (b_ref[...] / jnp.sum(sums_ref[...], axis=0))

    def step(i, z, cols):
        ref = blocks_vmem.at[i]
        factor = jnp.exp(block_shift(ref, z, sub, nl) - far) * col
        plan = [block_part(ref, z, sub, n) * factor[n : n + 1] for n in range(nl)]
        row = a / jnp.sum(functools.reduce(jnp.add, plan), axis=1, keepdims=True)
        side = yl if i < 2 else 1 - yl
        start = pl.multiple_of((i % 2 * 2 + side) * rows + z * sub, sub)
        sums = []
        for n in range(nh):
            part = jnp.where(c == 0, plan[n], plan[nh + n]) * row
            sums.append(cols[n] + group_sum(part))
            lane = n * LANES
            plan_ref[pl.ds(start, sub), lane : lane + LANES] = part.astype(jnp.bfloat16)
        return tuple(sums)

    cols = (jnp.zeros((8, LANES), jnp.float32),) * nh
    for i in range(len(sources)):
        loads[i].wait()
        cols = lax.fori_loop(0, nz, functools.partial(step, i), cols, unroll=2)

    half = nh * LANES
    for copy in copies:
        copy.wait()
    mixed = lax.dot_general(
        plan_ref[...],
        train_vmem[...].reshape(4 * rows, train_ref.shape[1]),
        (((0,), (0,)), ((), ())),
        preferred_element_type=jnp.float32,
    )
    nchips = out_ref.shape[0]
    mine = half // nchips
    parts = lane_blocks(mixed.astype(jnp.bfloat16))
    for n, part in enumerate(parts):
        out_ref[:, n * mine : (n + 1) * mine, :] = part.reshape(nchips, mine, LANES)
    per = LANES // mine
    for n in range(nh):
        total = jnp.sum(cols[n], axis=0, keepdims=True)
        tail = stack_rows(split3(total), MIXTURE_TAIL).astype(jnp.bfloat16)
        out_ref[n * per : (n + 1) * per, len(parts) * mine :, :] = jnp.broadcast_to(
            tail[None], (per, MIXTURE_TAIL, LANES)
        )


def output_kernel(place_ref, got_ref, out_ref):
    mine, feats = out_ref.shape
    nl = feats // LANES
    total = jnp.sum(got_ref[...].astype(jnp.float32), axis=0)
    mass = total[nl * mine : nl * mine + 1] + (
        total[nl * mine + 1 : nl * mine + 2] + total[nl * mine + 2 : nl * mine + 3]
    )
    lane = lax.broadcasted_iota(jnp.int32, (mine, LANES), 1)
    target = lax.broadcasted_iota(jnp.int32, (mine, LANES), 0) + place_ref[2] * mine
    mass = jnp.sum(jnp.where(lane == target, mass, 0.0), axis=1, keepdims=True)
    for n in range(nl):
        part = total[n * mine : (n + 1) * mine] / mass
        out_ref[:, n * LANES : (n + 1) * LANES] = part.astype(jnp.bfloat16)


def shards(train, target, mass):
    rows, feats = train.shape
    nc = lax.axis_size("c")
    nchips = lax.axis_size(CHIPS)
    nex = nc * nchips
    nz = lax.axis_size("z")
    nf = lax.axis_size(FEAT)
    mine = target.shape[0]
    nt = mine * nex
    nl = nt // LANES
    half = nt // nc
    sub = rows // nf
    scale = 3.0 / math.sqrt(F)
    a = 1.0 / (rows * nex)
    full = pl.BlockSpec(memory_space=VMEM)
    anywhere = pl.BlockSpec(memory_space=pl.ANY)
    scalars = pl.BlockSpec(memory_space=pltpu.SMEM)

    core_train = lax.ppermute(train, "c", SWAP)

    same_core = spread(target, CHIPS, nchips).reshape(nchips * mine, feats)
    mass = mass.reshape(nchips, nc, mine).transpose(1, 0, 2).reshape(nl, LANES)
    targets = spread(same_core, "c", nc).reshape(nt, feats)

    codes = pl.pallas_call(
        functools.partial(encode_kernel, sub),
        out_shape=jax.ShapeDtypeStruct((nf, nl * sub + CODE_TAIL, LANES), jnp.bfloat16),
        in_specs=[full] * 2,
        out_specs=full,
        scratch_shapes=[VMEM((2, 4 * sub, nt), jnp.float32)],
        compiler_params=MIDDLE,
    )(train, targets)
    codes = lax.all_to_all(codes, PIECES, 0, 0, tiled=True)
    blocks = pl.pallas_call(
        functools.partial(rows_kernel, sub, scale),
        out_shape=jax.ShapeDtypeStruct((nz, nl * sub + KERNEL_TAIL, LANES), jnp.bfloat16),
        in_specs=[full],
        out_specs=full,
        scratch_shapes=[VMEM((sub, nt), jnp.float32)],
        compiler_params=MIDDLE,
    )(codes)

    own = lax.all_to_all(blocks, "z", 0, 0, tiled=True)
    other = lax.ppermute(own, "yl", SWAP)
    core_own = lax.ppermute(own, "c", SWAP)

    def copies(axes):
        return jax.ShapeDtypeStruct((lax.axis_size(axes), nl, LANES), jnp.float32)

    vector = jax.ShapeDtypeStruct((nl, LANES), jnp.float32)
    stats = pl.pallas_call(
        functools.partial(statistics_kernel, sub),
        out_shape=copies(ROWS),
        in_specs=[full],
        out_specs=full,
        compiler_params=SMALL,
    )(own)
    stats = lax.all_to_all(stats, ROWS, 0, 0, tiled=True)
    far, col, b, sums = pl.pallas_call(
        functools.partial(columns_kernel, sub, a),
        out_shape=(vector, vector, vector, copies(CHIP_ROWS)),
        in_specs=[full] * 4,
        out_specs=(full,) * 4,
        compiler_params=SMALL,
    )(stats, own, core_own, mass)
    sums = lax.all_to_all(sums, CHIP_ROWS, 0, 0, tiled=True)
    other_copy = pl.pallas_call(
        copy_kernel,
        out_shape=jax.ShapeDtypeStruct(other.shape, other.dtype),
        in_specs=[full],
        out_specs=full,
        compiler_params=SMALL,
    )(other)
    core_other = lax.ppermute(other_copy, "c", SWAP)

    slot = jnp.bitwise_and(lax.axis_index(CHIPS), LANES // mine - 1)
    place = jnp.stack([lax.axis_index("c"), lax.axis_index("yl"), slot]).astype(jnp.int32)
    block = feats // LANES * mine + MIXTURE_TAIL
    send = pl.pallas_call(
        functools.partial(mixture_kernel, sub, a),
        out_shape=jax.ShapeDtypeStruct((nchips, block, LANES), jnp.bfloat16),
        in_specs=[scalars] + [full] * 4 + [anywhere] * 6,
        out_specs=full,
        scratch_shapes=[
            VMEM((nc * rows, half), jnp.bfloat16),
            VMEM((4,) + own.shape, jnp.bfloat16),
            VMEM((2, rows, feats), jnp.bfloat16),
            pltpu.SemaphoreType.DMA((6,)),
        ],
        compiler_params=LARGE,
    )(place, sums, far, col, b, own, other, core_own, core_other, train, core_train)
    got = lax.all_to_all(send, CHIPS, 0, 0, tiled=True)
    return pl.pallas_call(
        output_kernel,
        out_shape=jax.ShapeDtypeStruct((mine, feats), jnp.bfloat16),
        in_specs=[scalars, full],
        out_specs=full,
        compiler_params=SMALL,
    )(place, got)


def solution(mesh):
    fine = Mesh(mesh.devices.reshape(4, 4, 2, 8, 2), ("yh", "x", "c", "z", "yl"))

    return jax.shard_map(
        shards,
        mesh=fine,
        in_specs=(P(EX, FEAT), P(EX, FEAT), P()),
        out_specs=P(EX, FEAT),
        check_vma=False,
    )
```

```python
import functools
import math

import jax
import jax.numpy as jnp
from jax import lax
from jax.experimental import pallas as pl
from jax.experimental.pallas import tpu as pltpu
from jax.sharding import Mesh, PartitionSpec as P


F = 16384
CHIPS = ("x", "yh")
EX = ("yh", "x", "c")
FEAT = ("z", "yl")
PIECES = ("yl", "z")
ROWS = ("yh", "x", "c", "yl")
CHIP_ROWS = ("yh", "x", "yl")
LANES = 128
CODE_TAIL = 8
KERNEL_TAIL = 16
MIXTURE_TAIL = 8
SWAP = [(0, 1), (1, 0)]
VMEM = pltpu.VMEM
MIDDLE = pltpu.CompilerParams(vmem_limit_bytes=12 * 2**20)
SMALL = pltpu.CompilerParams(vmem_limit_bytes=4 * 2**20)
LARGE = pltpu.CompilerParams(vmem_limit_bytes=24 * 2**20)


SPAN = 249.0
BASE = 124.0


def round_up(v):
    return (v * (1.0 + 2.0**-7)).astype(jnp.bfloat16).astype(jnp.float32)


def split3(v):
    hi = v.astype(jnp.bfloat16).astype(jnp.float32)
    mid = (v - hi).astype(jnp.bfloat16).astype(jnp.float32)
    return hi, mid, v - hi - mid


def stack_rows(rows, height):
    index = lax.broadcasted_iota(jnp.int32, (height, LANES), 0)
    out = jnp.zeros((height, LANES), jnp.float32)
    for k, row in enumerate(rows):
        out = jnp.where(index == k, row, out)
    return out


def lane_blocks(v):
    return [v[:, k : k + LANES] for k in range(0, v.shape[1], LANES)]


def diagonal(sub):
    return lax.broadcasted_iota(jnp.int32, (sub, LANES), 0) == (
        lax.broadcasted_iota(jnp.int32, (sub, LANES), 1)
    )


def encode_kernel(sub, train_ref, targets_ref, out_ref, partial_ref):
    rows = train_ref.shape[0]
    step = partial_ref.shape[1]
    on_diagonal = diagonal(sub)
    for start in range(0, rows, step):
        slot = start // step % 2
        partial_ref[slot] = lax.dot_general(
            train_ref[start : start + step, :],
            targets_ref[...],
            (((1,), (1,)), ((), ())),
            preferred_element_type=jnp.float32,
        )
        for j in range(step // sub):
            k = start // sub + j
            p = partial_ref[slot, j * sub : (j + 1) * sub, :]
            high = jnp.max(p, axis=1, keepdims=True)
            low = jnp.min(p, axis=1, keepdims=True)
            p = p - 0.5 * (high + low)
            wide = jnp.max(jnp.abs(p), axis=1, keepdims=True)
            row = round_up(jnp.maximum(wide, 1e-30))
            p = p * (1.0 / row)
            col = round_up(jnp.maximum(jnp.max(jnp.abs(p), axis=0, keepdims=True), 1e-30))
            u = p * (1.0 / col)
            code = jnp.exp2(jnp.abs(u) * SPAN - BASE)
            code = jnp.where(u < 0, -code, code).astype(jnp.bfloat16)
            parts = lane_blocks(code)
            for n, part in enumerate(parts):
                out_ref[k, n * sub : (n + 1) * sub, :] = part
            row = jnp.sum(jnp.where(on_diagonal, row, 0.0), axis=0, keepdims=True)
            tail = stack_rows(lane_blocks(col) + [row], CODE_TAIL)
            out_ref[k, len(parts) * sub :, :] = tail.astype(jnp.bfloat16)


def rows_kernel(sub, scale, codes_ref, out_ref, logits_ref):
    nf = codes_ref.shape[0]
    nz = out_ref.shape[0]
    nl = logits_ref.shape[1] // LANES
    on_diagonal = diagonal(sub)
    tails, rows = [], []
    for k in range(nf):
        tail = codes_ref[k, nl * sub :, :].astype(jnp.float32)
        tails.append(tail * (scale / SPAN))
        row = jnp.where(on_diagonal, tail[nl : nl + 1, :], 0.0)
        rows.append(jnp.sum(row, axis=1, keepdims=True))
    for n in range(nl):
        total = jnp.zeros((sub, LANES), jnp.float32)
        for k in range(nf):
            code = codes_ref[k, n * sub : (n + 1) * sub, :].astype(jnp.float32)
            size = jnp.log(jnp.abs(code)) * (1.0 / math.log(2.0)) + BASE
            size = jnp.where(code < 0, -size, size)
            total += size * tails[k][n : n + 1, :] * rows[k]
        logits_ref[:, n * LANES : (n + 1) * LANES] = total

    logits = logits_ref[...]
    top = jnp.max(logits, axis=1, keepdims=True)
    v = logits - top
    v = v - jnp.log(jnp.sum(jnp.exp(v), axis=1, keepdims=True))
    shift = jnp.max(v, axis=0, keepdims=True)
    kern = lane_blocks(jnp.exp(v - shift).astype(jnp.bfloat16))
    terms = [row for term in split3(shift) for row in lane_blocks(term)]
    tail = stack_rows(terms, KERNEL_TAIL).astype(jnp.bfloat16)
    for z in range(nz):
        for n, part in enumerate(kern):
            out_ref[z, n * sub : (n + 1) * sub, :] = part
        out_ref[z, nl * sub :, :] = tail


def spread(block, axes, n):
    copies = jnp.broadcast_to(block[None], (n,) + block.shape)
    return lax.all_to_all(copies, axes, 0, 0, tiled=True)


def block_shift(ref, z, sub, nl):
    tail = ref[z, nl * sub :, :].astype(jnp.float32)
    return tail[:nl] + tail[nl : 2 * nl] + tail[2 * nl : 3 * nl]


def block_part(ref, z, sub, n):
    return ref[z, n * sub : (n + 1) * sub, :].astype(jnp.float32)


def group_sum(v):
    return functools.reduce(jnp.add, [v[k : k + 8] for k in range(0, v.shape[0], 8)])


def statistics_kernel(sub, own_ref, out_ref):
    nz = own_ref.shape[0]
    nl = out_ref.shape[1]
    shifts = [block_shift(own_ref, z, sub, nl) for z in range(nz)]
    top = functools.reduce(jnp.maximum, shifts)
    total = [jnp.zeros((8, LANES), jnp.float32)] * nl
    for z in range(nz):
        factor = jnp.exp(shifts[z] - top)
        for n in range(nl):
            part = group_sum(block_part(own_ref, z, sub, n))
            total[n] = total[n] + factor[n : n + 1] * part
    total = [jnp.sum(t, axis=0, keepdims=True) for t in total]
    log_sum = top + jnp.log(stack_rows(total, nl))
    out_ref[...] = jnp.broadcast_to(log_sum[None], out_ref.shape)


def columns_kernel(sub, a, stats_ref, own_ref, core_ref, mass_ref, far_ref, col_ref, b_ref, out_ref):
    nz = own_ref.shape[0]
    nl = out_ref.shape[1]
    stats = stats_ref[...]
    far = jnp.max(stats, axis=0)
    b = mass_ref[...] / jnp.sum(mass_ref[...])
    col = b / jnp.sum(jnp.exp(stats - far[None]), axis=0)
    cols = [jnp.zeros((8, LANES), jnp.float32)] * nl
    for z in range(nz):
        for ref in (own_ref, core_ref):
            factor = jnp.exp(block_shift(ref, z, sub, nl) - far) * col
            plan = [block_part(ref, z, sub, n) * factor[n : n + 1] for n in range(nl)]
            row = a / jnp.sum(functools.reduce(jnp.add, plan), axis=1, keepdims=True)
            for n in range(nl):
                cols[n] = cols[n] + group_sum(plan[n] * row)
    cols = [jnp.sum(t, axis=0, keepdims=True) for t in cols]
    far_ref[...] = far
    b_ref[...] = b
    col_ref[...] = col
    out_ref[...] = jnp.broadcast_to(stack_rows(cols, nl)[None], out_ref.shape)


def copy_kernel(in_ref, out_ref):
    out_ref[...] = in_ref[...]


def mixture_kernel(
    sub,
    a,
    place_ref,
    sums_ref,
    far_ref,
    col_ref,
    b_ref,
    own_ref,
    other_ref,
    core_own_ref,
    core_other_ref,
    train_ref,
    core_train_ref,
    out_ref,
    plan_ref,
    blocks_vmem,
    train_vmem,
    sems,
):
    _, nz, _, _ = blocks_vmem.shape
    nl = sums_ref.shape[1]
    nh = nl // 2
    rows = nz * sub
    c, yl = place_ref[0], place_ref[1]
    sources = (own_ref, core_own_ref, other_ref, core_other_ref)
    loads = [
        pltpu.make_async_copy(src, blocks_vmem.at[k], sems.at[k])
        for k, src in enumerate(sources)
    ]
    copies = [
        pltpu.make_async_copy(src, train_vmem.at[k], sems.at[len(sources) + k])
        for k, src in enumerate((train_ref, core_train_ref))
    ]
    for copy in loads + copies:
        copy.start()
    far = far_ref[...]
    col = col_ref[...] * (b_ref[...] / jnp.sum(sums_ref[...], axis=0))

    def step(i, z, cols):
        ref = blocks_vmem.at[i]
        factor = jnp.exp(block_shift(ref, z, sub, nl) - far) * col
        plan = [block_part(ref, z, sub, n) * factor[n : n + 1] for n in range(nl)]
        row = a / jnp.sum(functools.reduce(jnp.add, plan), axis=1, keepdims=True)
        side = yl if i < 2 else 1 - yl
        start = pl.multiple_of((i % 2 * 2 + side) * rows + z * sub, sub)
        sums = []
        for n in range(nh):
            part = jnp.where(c == 0, plan[n], plan[nh + n]) * row
            sums.append(cols[n] + group_sum(part))
            lane = n * LANES
            plan_ref[pl.ds(start, sub), lane : lane + LANES] = part.astype(jnp.bfloat16)
        return tuple(sums)

    cols = (jnp.zeros((8, LANES), jnp.float32),) * nh
    for i in range(len(sources)):
        loads[i].wait()
        cols = lax.fori_loop(0, nz, functools.partial(step, i), cols, unroll=2)

    half = nh * LANES
    for copy in copies:
        copy.wait()
    mixed = lax.dot_general(
        plan_ref[...],
        train_vmem[...].reshape(4 * rows, train_ref.shape[1]),
        (((0,), (0,)), ((), ())),
        preferred_element_type=jnp.float32,
    )
    nchips = out_ref.shape[0]
    mine = half // nchips
    parts = lane_blocks(mixed.astype(jnp.bfloat16))
    for n, part in enumerate(parts):
        out_ref[:, n * mine : (n + 1) * mine, :] = part.reshape(nchips, mine, LANES)
    per = LANES // mine
    for n in range(nh):
        total = jnp.sum(cols[n], axis=0, keepdims=True)
        tail = stack_rows(split3(total), MIXTURE_TAIL).astype(jnp.bfloat16)
        out_ref[n * per : (n + 1) * per, len(parts) * mine :, :] = jnp.broadcast_to(
            tail[None], (per, MIXTURE_TAIL, LANES)
        )


def output_kernel(place_ref, got_ref, out_ref):
    mine, feats = out_ref.shape
    nl = feats // LANES
    total = jnp.sum(got_ref[...].astype(jnp.float32), axis=0)
    mass = total[nl * mine : nl * mine + 1] + (
        total[nl * mine + 1 : nl * mine + 2] + total[nl * mine + 2 : nl * mine + 3]
    )
    lane = lax.broadcasted_iota(jnp.int32, (mine, LANES), 1)
    target = lax.broadcasted_iota(jnp.int32, (mine, LANES), 0) + place_ref[2] * mine
    mass = jnp.sum(jnp.where(lane == target, mass, 0.0), axis=1, keepdims=True)
    for n in range(nl):
        part = total[n * mine : (n + 1) * mine] / mass
        out_ref[:, n * LANES : (n + 1) * LANES] = part.astype(jnp.bfloat16)


def shards(train, target, mass):
    rows, feats = train.shape
    nc = lax.axis_size("c")
    nchips = lax.axis_size(CHIPS)
    nex = nc * nchips
    nz = lax.axis_size("z")
    nf = lax.axis_size(FEAT)
    mine = target.shape[0]
    nt = mine * nex
    nl = nt // LANES
    half = nt // nc
    sub = rows // nf
    scale = 3.0 / math.sqrt(F)
    a = 1.0 / (rows * nex)
    full = pl.BlockSpec(memory_space=VMEM)
    anywhere = pl.BlockSpec(memory_space=pl.ANY)
    scalars = pl.BlockSpec(memory_space=pltpu.SMEM)

    core_train = lax.ppermute(train, "c", SWAP)

    same_core = spread(target, CHIPS, nchips).reshape(nchips * mine, feats)
    mass = mass.reshape(lax.axis_size("yh"), lax.axis_size("x"), nc, mine)
    mass = mass.transpose(2, 1, 0, 3).reshape(nl, LANES)
    targets = spread(same_core, "c", nc).reshape(nt, feats)

    codes = pl.pallas_call(
        functools.partial(encode_kernel, sub),
        out_shape=jax.ShapeDtypeStruct((nf, nl * sub + CODE_TAIL, LANES), jnp.bfloat16),
        in_specs=[full] * 2,
        out_specs=full,
        scratch_shapes=[VMEM((2, 4 * sub, nt), jnp.float32)],
        compiler_params=MIDDLE,
    )(train, targets)
    codes = lax.all_to_all(codes, PIECES, 0, 0, tiled=True)
    blocks = pl.pallas_call(
        functools.partial(rows_kernel, sub, scale),
        out_shape=jax.ShapeDtypeStruct((nz, nl * sub + KERNEL_TAIL, LANES), jnp.bfloat16),
        in_specs=[full],
        out_specs=full,
        scratch_shapes=[VMEM((sub, nt), jnp.float32)],
        compiler_params=MIDDLE,
    )(codes)

    own = lax.all_to_all(blocks, "z", 0, 0, tiled=True)
    other = lax.ppermute(own, "yl", SWAP)
    core_own = lax.ppermute(own, "c", SWAP)

    def copies(axes):
        return jax.ShapeDtypeStruct((lax.axis_size(axes), nl, LANES), jnp.float32)

    vector = jax.ShapeDtypeStruct((nl, LANES), jnp.float32)
    stats = pl.pallas_call(
        functools.partial(statistics_kernel, sub),
        out_shape=copies(ROWS),
        in_specs=[full],
        out_specs=full,
        compiler_params=SMALL,
    )(own)
    stats = lax.all_to_all(stats, ROWS, 0, 0, tiled=True)
    far, col, b, sums = pl.pallas_call(
        functools.partial(columns_kernel, sub, a),
        out_shape=(vector, vector, vector, copies(CHIP_ROWS)),
        in_specs=[full] * 4,
        out_specs=(full,) * 4,
        compiler_params=SMALL,
    )(stats, own, core_own, mass)
    sums = lax.all_to_all(sums, CHIP_ROWS, 0, 0, tiled=True)
    other_copy = pl.pallas_call(
        copy_kernel,
        out_shape=jax.ShapeDtypeStruct(other.shape, other.dtype),
        in_specs=[full],
        out_specs=full,
        compiler_params=SMALL,
    )(other)
    core_other = lax.ppermute(other_copy, "c", SWAP)

    slot = jnp.bitwise_and(lax.axis_index(CHIPS), LANES // mine - 1)
    place = jnp.stack([lax.axis_index("c"), lax.axis_index("yl"), slot]).astype(jnp.int32)
    block = feats // LANES * mine + MIXTURE_TAIL
    send = pl.pallas_call(
        functools.partial(mixture_kernel, sub, a),
        out_shape=jax.ShapeDtypeStruct((nchips, block, LANES), jnp.bfloat16),
        in_specs=[scalars] + [full] * 4 + [anywhere] * 6,
        out_specs=full,
        scratch_shapes=[
            VMEM((nc * rows, half), jnp.bfloat16),
            VMEM((4,) + own.shape, jnp.bfloat16),
            VMEM((2, rows, feats), jnp.bfloat16),
            pltpu.SemaphoreType.DMA((6,)),
        ],
        compiler_params=LARGE,
    )(place, sums, far, col, b, own, other, core_own, core_other, train, core_train)
    got = lax.all_to_all(send, CHIPS, 0, 0, tiled=True)
    return pl.pallas_call(
        output_kernel,
        out_shape=jax.ShapeDtypeStruct((mine, feats), jnp.bfloat16),
        in_specs=[scalars, full],
        out_specs=full,
        compiler_params=SMALL,
    )(place, got)


def solution(mesh):
    fine = Mesh(mesh.devices.reshape(4, 4, 2, 8, 2), ("yh", "x", "c", "z", "yl"))

    return jax.shard_map(
        shards,
        mesh=fine,
        in_specs=(P(EX, FEAT), P(EX, FEAT), P()),
        out_specs=P(EX, FEAT),
        check_vma=False,
    )
```

```python
import functools
import math

import jax
import jax.numpy as jnp
from jax import lax
from jax.experimental import pallas as pl
from jax.experimental.pallas import tpu as pltpu
from jax.sharding import Mesh, PartitionSpec as P


F = 16384
CHIPS = ("x", "yh")
EX = ("yh", "x", "c")
FEAT = ("z", "yl")
PIECES = ("yl", "z")
ROWS = ("x", "yh", "yl", "c")
CHIP_ROWS = ("x", "yh", "yl")
LANES = 128
CODE_TAIL = 8
KERNEL_TAIL = 16
MIXTURE_TAIL = 8
SWAP = [(0, 1), (1, 0)]
VMEM = pltpu.VMEM
MIDDLE = pltpu.CompilerParams(vmem_limit_bytes=12 * 2**20)
SMALL = pltpu.CompilerParams(vmem_limit_bytes=4 * 2**20)
LARGE = pltpu.CompilerParams(vmem_limit_bytes=24 * 2**20)


SPAN = 249.0
BASE = 124.0


def round_up(v):
    return (v * (1.0 + 2.0**-7)).astype(jnp.bfloat16).astype(jnp.float32)


def split3(v):
    hi = v.astype(jnp.bfloat16).astype(jnp.float32)
    mid = (v - hi).astype(jnp.bfloat16).astype(jnp.float32)
    return hi, mid, v - hi - mid


def stack_rows(rows, height):
    index = lax.broadcasted_iota(jnp.int32, (height, LANES), 0)
    out = jnp.zeros((height, LANES), jnp.float32)
    for k, row in enumerate(rows):
        out = jnp.where(index == k, row, out)
    return out


def lane_blocks(v):
    return [v[:, k : k + LANES] for k in range(0, v.shape[1], LANES)]


def diagonal(sub):
    return lax.broadcasted_iota(jnp.int32, (sub, LANES), 0) == (
        lax.broadcasted_iota(jnp.int32, (sub, LANES), 1)
    )


def encode_kernel(sub, train_ref, targets_ref, out_ref, partial_ref):
    rows = train_ref.shape[0]
    step = partial_ref.shape[1]
    on_diagonal = diagonal(sub)
    for start in range(0, rows, step):
        slot = start // step % 2
        partial_ref[slot] = lax.dot_general(
            train_ref[start : start + step, :],
            targets_ref[...],
            (((1,), (1,)), ((), ())),
            preferred_element_type=jnp.float32,
        )
        for j in range(step // sub):
            k = start // sub + j
            p = partial_ref[slot, j * sub : (j + 1) * sub, :]
            high = jnp.max(p, axis=1, keepdims=True)
            low = jnp.min(p, axis=1, keepdims=True)
            p = p - 0.5 * (high + low)
            wide = jnp.max(jnp.abs(p), axis=1, keepdims=True)
            row = round_up(jnp.maximum(wide, 1e-30))
            p = p * (1.0 / row)
            col = round_up(jnp.maximum(jnp.max(jnp.abs(p), axis=0, keepdims=True), 1e-30))
            u = p * (1.0 / col)
            code = jnp.exp2(jnp.abs(u) * SPAN - BASE)
            code = jnp.where(u < 0, -code, code).astype(jnp.bfloat16)
            parts = lane_blocks(code)
            for n, part in enumerate(parts):
                out_ref[k, n * sub : (n + 1) * sub, :] = part
            row = jnp.sum(jnp.where(on_diagonal, row, 0.0), axis=0, keepdims=True)
            tail = stack_rows(lane_blocks(col) + [row], CODE_TAIL)
            out_ref[k, len(parts) * sub :, :] = tail.astype(jnp.bfloat16)


def rows_kernel(sub, scale, codes_ref, out_ref, logits_ref):
    nf = codes_ref.shape[0]
    nz = out_ref.shape[0]
    nl = logits_ref.shape[1] // LANES
    on_diagonal = diagonal(sub)
    tails, rows = [], []
    for k in range(nf):
        tail = codes_ref[k, nl * sub :, :].astype(jnp.float32)
        tails.append(tail * (scale / SPAN))
        row = jnp.where(on_diagonal, tail[nl : nl + 1, :], 0.0)
        rows.append(jnp.sum(row, axis=1, keepdims=True))
    for n in range(nl):
        total = jnp.zeros((sub, LANES), jnp.float32)
        for k in range(nf):
            code = codes_ref[k, n * sub : (n + 1) * sub, :].astype(jnp.float32)
            size = jnp.log(jnp.abs(code)) * (1.0 / math.log(2.0)) + BASE
            size = jnp.where(code < 0, -size, size)
            total += size * tails[k][n : n + 1, :] * rows[k]
        logits_ref[:, n * LANES : (n + 1) * LANES] = total

    logits = logits_ref[...]
    top = jnp.max(logits, axis=1, keepdims=True)
    v = logits - top
    v = v - jnp.log(jnp.sum(jnp.exp(v), axis=1, keepdims=True))
    shift = jnp.max(v, axis=0, keepdims=True)
    kern = lane_blocks(jnp.exp(v - shift).astype(jnp.bfloat16))
    terms = [row for term in split3(shift) for row in lane_blocks(term)]
    tail = stack_rows(terms, KERNEL_TAIL).astype(jnp.bfloat16)
    for z in range(nz):
        for n, part in enumerate(kern):
            out_ref[z, n * sub : (n + 1) * sub, :] = part
        out_ref[z, nl * sub :, :] = tail


def spread(block, axes, n):
    copies = jnp.broadcast_to(block[None], (n,) + block.shape)
    return lax.all_to_all(copies, axes, 0, 0, tiled=True)


def block_shift(ref, z, sub, nl):
    tail = ref[z, nl * sub :, :].astype(jnp.float32)
    return tail[:nl] + tail[nl : 2 * nl] + tail[2 * nl : 3 * nl]


def block_part(ref, z, sub, n):
    return ref[z, n * sub : (n + 1) * sub, :].astype(jnp.float32)


def group_sum(v):
    return functools.reduce(jnp.add, [v[k : k + 8] for k in range(0, v.shape[0], 8)])


def statistics_kernel(sub, own_ref, out_ref):
    nz = own_ref.shape[0]
    nl = out_ref.shape[1]
    shifts = [block_shift(own_ref, z, sub, nl) for z in range(nz)]
    top = functools.reduce(jnp.maximum, shifts)
    total = [jnp.zeros((8, LANES), jnp.float32)] * nl
    for z in range(nz):
        factor = jnp.exp(shifts[z] - top)
        for n in range(nl):
            part = group_sum(block_part(own_ref, z, sub, n))
            total[n] = total[n] + factor[n : n + 1] * part
    total = [jnp.sum(t, axis=0, keepdims=True) for t in total]
    log_sum = top + jnp.log(stack_rows(total, nl))
    out_ref[...] = jnp.broadcast_to(log_sum[None], out_ref.shape)


def columns_kernel(sub, a, stats_ref, own_ref, core_ref, mass_ref, far_ref, col_ref, b_ref, out_ref):
    nz = own_ref.shape[0]
    nl = out_ref.shape[1]
    stats = stats_ref[...]
    far = jnp.max(stats, axis=0)
    b = mass_ref[...] / jnp.sum(mass_ref[...])
    col = b / jnp.sum(jnp.exp(stats - far[None]), axis=0)
    cols = [jnp.zeros((8, LANES), jnp.float32)] * nl
    for z in range(nz):
        for ref in (own_ref, core_ref):
            factor = jnp.exp(block_shift(ref, z, sub, nl) - far) * col
            plan = [block_part(ref, z, sub, n) * factor[n : n + 1] for n in range(nl)]
            row = a / jnp.sum(functools.reduce(jnp.add, plan), axis=1, keepdims=True)
            for n in range(nl):
                cols[n] = cols[n] + group_sum(plan[n] * row)
    cols = [jnp.sum(t, axis=0, keepdims=True) for t in cols]
    far_ref[...] = far
    b_ref[...] = b
    col_ref[...] = col
    out_ref[...] = jnp.broadcast_to(stack_rows(cols, nl)[None], out_ref.shape)


def copy_kernel(in_ref, out_ref):
    out_ref[...] = in_ref[...]


def mixture_kernel(
    sub,
    a,
    place_ref,
    sums_ref,
    far_ref,
    col_ref,
    b_ref,
    own_ref,
    core_own_ref,
    other_ref,
    core_other_ref,
    train_ref,
    core_train_ref,
    out_ref,
    plan_ref,
    blocks_vmem,
    train_vmem,
    sems,
):
    _, nz, _, _ = blocks_vmem.shape
    nl = sums_ref.shape[1]
    nh = nl // 2
    rows = nz * sub
    c, yl = place_ref[0], place_ref[1]
    late = (other_ref, core_other_ref)
    loads = [
        pltpu.make_async_copy(src, blocks_vmem.at[k], sems.at[k])
        for k, src in enumerate(late)
    ]
    sources = (own_ref, core_own_ref, blocks_vmem.at[0], blocks_vmem.at[1])
    copies = [
        pltpu.make_async_copy(src, train_vmem.at[k], sems.at[len(late) + k])
        for k, src in enumerate((train_ref, core_train_ref))
    ]
    for copy in loads + copies:
        copy.start()
    far = far_ref[...]
    col = col_ref[...] * (b_ref[...] / jnp.sum(sums_ref[...], axis=0))

    def step(i, z, cols):
        ref = sources[i]
        factor = jnp.exp(block_shift(ref, z, sub, nl) - far) * col
        plan = [block_part(ref, z, sub, n) * factor[n : n + 1] for n in range(nl)]
        row = a / jnp.sum(functools.reduce(jnp.add, plan), axis=1, keepdims=True)
        side = yl if i < 2 else 1 - yl
        start = pl.multiple_of((i % 2 * 2 + side) * rows + z * sub, sub)
        sums = []
        for n in range(nh):
            part = jnp.where(c == 0, plan[n], plan[nh + n]) * row
            sums.append(cols[n] + group_sum(part))
            lane = n * LANES
            plan_ref[pl.ds(start, sub), lane : lane + LANES] = part.astype(jnp.bfloat16)
        return tuple(sums)

    cols = (jnp.zeros((8, LANES), jnp.float32),) * nh
    for i in range(len(sources)):
        if i >= 2:
            loads[i - 2].wait()
        cols = lax.fori_loop(0, nz, functools.partial(step, i), cols, unroll=2)

    half = nh * LANES
    for copy in copies:
        copy.wait()
    mixed = lax.dot_general(
        plan_ref[...],
        train_vmem[...].reshape(4 * rows, train_ref.shape[1]),
        (((0,), (0,)), ((), ())),
        preferred_element_type=jnp.float32,
    )
    nchips = out_ref.shape[0]
    mine = half // nchips
    parts = lane_blocks(mixed.astype(jnp.bfloat16))
    for n, part in enumerate(parts):
        out_ref[:, n * mine : (n + 1) * mine, :] = part.reshape(nchips, mine, LANES)
    per = LANES // mine
    for n in range(nh):
        total = jnp.sum(cols[n], axis=0, keepdims=True)
        tail = stack_rows(split3(total), MIXTURE_TAIL).astype(jnp.bfloat16)
        out_ref[n * per : (n + 1) * per, len(parts) * mine :, :] = jnp.broadcast_to(
            tail[None], (per, MIXTURE_TAIL, LANES)
        )


def output_kernel(place_ref, got_ref, out_ref):
    mine, feats = out_ref.shape
    nl = feats // LANES
    total = jnp.sum(got_ref[...].astype(jnp.float32), axis=0)
    mass = total[nl * mine : nl * mine + 1] + (
        total[nl * mine + 1 : nl * mine + 2] + total[nl * mine + 2 : nl * mine + 3]
    )
    lane = lax.broadcasted_iota(jnp.int32, (mine, LANES), 1)
    target = lax.broadcasted_iota(jnp.int32, (mine, LANES), 0) + place_ref[2] * mine
    mass = jnp.sum(jnp.where(lane == target, mass, 0.0), axis=1, keepdims=True)
    for n in range(nl):
        part = total[n * mine : (n + 1) * mine] / mass
        out_ref[:, n * LANES : (n + 1) * LANES] = part.astype(jnp.bfloat16)


def shards(train, target, mass):
    rows, feats = train.shape
    nc = lax.axis_size("c")
    nchips = lax.axis_size(CHIPS)
    nex = nc * nchips
    nz = lax.axis_size("z")
    nf = lax.axis_size(FEAT)
    mine = target.shape[0]
    nt = mine * nex
    nl = nt // LANES
    half = nt // nc
    sub = rows // nf
    scale = 3.0 / math.sqrt(F)
    a = 1.0 / (rows * nex)
    full = pl.BlockSpec(memory_space=VMEM)
    anywhere = pl.BlockSpec(memory_space=pl.ANY)
    scalars = pl.BlockSpec(memory_space=pltpu.SMEM)

    core_train = lax.ppermute(train, "c", SWAP)

    same_core = spread(target, CHIPS, nchips).reshape(nchips * mine, feats)
    mass = mass.reshape(lax.axis_size("yh"), lax.axis_size("x"), nc, mine)
    mass = mass.transpose(2, 1, 0, 3).reshape(nl, LANES)
    targets = spread(same_core, "c", nc).reshape(nt, feats)

    codes = pl.pallas_call(
        functools.partial(encode_kernel, sub),
        out_shape=jax.ShapeDtypeStruct((nf, nl * sub + CODE_TAIL, LANES), jnp.bfloat16),
        in_specs=[full] * 2,
        out_specs=full,
        scratch_shapes=[VMEM((2, 4 * sub, nt), jnp.float32)],
        compiler_params=MIDDLE,
    )(train, targets)
    codes = lax.all_to_all(codes, PIECES, 0, 0, tiled=True)
    blocks = pl.pallas_call(
        functools.partial(rows_kernel, sub, scale),
        out_shape=jax.ShapeDtypeStruct((nz, nl * sub + KERNEL_TAIL, LANES), jnp.bfloat16),
        in_specs=[full],
        out_specs=full,
        scratch_shapes=[VMEM((sub, nt), jnp.float32)],
        compiler_params=MIDDLE,
    )(codes)

    own = lax.all_to_all(blocks, "z", 0, 0, tiled=True)
    other = lax.ppermute(own, "yl", SWAP)
    core_own = lax.ppermute(own, "c", SWAP)

    def copies(axes):
        return jax.ShapeDtypeStruct((lax.axis_size(axes), nl, LANES), jnp.float32)

    vector = jax.ShapeDtypeStruct((nl, LANES), jnp.float32)
    stats = pl.pallas_call(
        functools.partial(statistics_kernel, sub),
        out_shape=copies(ROWS),
        in_specs=[full],
        out_specs=full,
        compiler_params=SMALL,
    )(own)
    stats = lax.all_to_all(stats, ROWS, 0, 0, tiled=True)
    far, col, b, sums = pl.pallas_call(
        functools.partial(columns_kernel, sub, a),
        out_shape=(vector, vector, vector, copies(CHIP_ROWS)),
        in_specs=[full] * 4,
        out_specs=(full,) * 4,
        compiler_params=SMALL,
    )(stats, own, core_own, mass)
    sums = lax.all_to_all(sums, CHIP_ROWS, 0, 0, tiled=True)
    other_copy = pl.pallas_call(
        copy_kernel,
        out_shape=jax.ShapeDtypeStruct(other.shape, other.dtype),
        in_specs=[full],
        out_specs=full,
        compiler_params=SMALL,
    )(other)
    core_other = lax.ppermute(other_copy, "c", SWAP)

    slot = jnp.bitwise_and(lax.axis_index(CHIPS), LANES // mine - 1)
    place = jnp.stack([lax.axis_index("c"), lax.axis_index("yl"), slot]).astype(jnp.int32)
    block = feats // LANES * mine + MIXTURE_TAIL
    send = pl.pallas_call(
        functools.partial(mixture_kernel, sub, a),
        out_shape=jax.ShapeDtypeStruct((nchips, block, LANES), jnp.bfloat16),
        in_specs=[scalars] + [full] * 6 + [anywhere] * 4,
        out_specs=full,
        scratch_shapes=[
            VMEM((nc * rows, half), jnp.bfloat16),
            VMEM((2,) + own.shape, jnp.bfloat16),
            VMEM((2, rows, feats), jnp.bfloat16),
            pltpu.SemaphoreType.DMA((4,)),
        ],
        compiler_params=LARGE,
    )(place, sums, far, col, b, own, core_own, other, core_other, train, core_train)
    got = lax.all_to_all(send, CHIPS, 0, 0, tiled=True)
    return pl.pallas_call(
        output_kernel,
        out_shape=jax.ShapeDtypeStruct((mine, feats), jnp.bfloat16),
        in_specs=[scalars, full],
        out_specs=full,
        compiler_params=SMALL,
    )(place, got)


def solution(mesh):
    fine = Mesh(mesh.devices.reshape(4, 4, 2, 8, 2), ("yh", "x", "c", "z", "yl"))

    return jax.shard_map(
        shards,
        mesh=fine,
        in_specs=(P(EX, FEAT), P(EX, FEAT), P()),
        out_specs=P(EX, FEAT),
        check_vma=False,
    )
```

```python
import functools
import math

import jax
import jax.numpy as jnp
from jax import lax
from jax.experimental import pallas as pl
from jax.experimental.pallas import tpu as pltpu
from jax.sharding import Mesh, PartitionSpec as P


F = 16384
CHIPS = ("x", "yh")
EX = ("yh", "x", "c")
FEAT = ("z", "yl")
PIECES = ("yl", "z")
ROWS = ("x", "yh", "yl", "c")
CHIP_ROWS = ("x", "yh", "yl")
LANES = 128
CODE_TAIL = 8
KERNEL_TAIL = 16
MIXTURE_TAIL = 8
SWAP = [(0, 1), (1, 0)]
VMEM = pltpu.VMEM
MIDDLE = pltpu.CompilerParams(vmem_limit_bytes=12 * 2**20)
SMALL = pltpu.CompilerParams(vmem_limit_bytes=4 * 2**20)
LARGE = pltpu.CompilerParams(vmem_limit_bytes=24 * 2**20)


SPAN = 249.0
BASE = 124.0


def round_up(v):
    return (v * (1.0 + 2.0**-7)).astype(jnp.bfloat16).astype(jnp.float32)


def split3(v):
    hi = v.astype(jnp.bfloat16).astype(jnp.float32)
    mid = (v - hi).astype(jnp.bfloat16).astype(jnp.float32)
    return hi, mid, v - hi - mid


def stack_rows(rows, height):
    index = lax.broadcasted_iota(jnp.int32, (height, LANES), 0)
    out = jnp.zeros((height, LANES), jnp.float32)
    for k, row in enumerate(rows):
        out = jnp.where(index == k, row, out)
    return out


def lane_blocks(v):
    return [v[:, k : k + LANES] for k in range(0, v.shape[1], LANES)]


def diagonal(sub):
    return lax.broadcasted_iota(jnp.int32, (sub, LANES), 0) == (
        lax.broadcasted_iota(jnp.int32, (sub, LANES), 1)
    )


def encode_kernel(sub, train_ref, targets_ref, out_ref, partial_ref):
    rows = train_ref.shape[0]
    step = partial_ref.shape[1]
    on_diagonal = diagonal(sub)
    for start in range(0, rows, step):
        slot = start // step % 2
        partial_ref[slot] = lax.dot_general(
            train_ref[start : start + step, :],
            targets_ref[...],
            (((1,), (1,)), ((), ())),
            preferred_element_type=jnp.float32,
        )
        for j in range(step // sub):
            k = start // sub + j
            p = partial_ref[slot, j * sub : (j + 1) * sub, :]
            high = jnp.max(p, axis=1, keepdims=True)
            low = jnp.min(p, axis=1, keepdims=True)
            p = p - 0.5 * (high + low)
            wide = jnp.max(jnp.abs(p), axis=1, keepdims=True)
            row = round_up(jnp.maximum(wide, 1e-30))
            p = p * (1.0 / row)
            col = round_up(jnp.maximum(jnp.max(jnp.abs(p), axis=0, keepdims=True), 1e-30))
            u = p * (1.0 / col)
            code = jnp.exp2(jnp.abs(u) * SPAN - BASE)
            code = jnp.where(u < 0, -code, code).astype(jnp.bfloat16)
            parts = lane_blocks(code)
            for n, part in enumerate(parts):
                out_ref[k, n * sub : (n + 1) * sub, :] = part
            row = jnp.sum(jnp.where(on_diagonal, row, 0.0), axis=0, keepdims=True)
            tail = stack_rows(lane_blocks(col) + [row], CODE_TAIL)
            out_ref[k, len(parts) * sub :, :] = tail.astype(jnp.bfloat16)


def rows_kernel(sub, scale, codes_ref, out_ref, logits_ref):
    nf = codes_ref.shape[0]
    nz = out_ref.shape[0]
    nl = logits_ref.shape[1] // LANES
    on_diagonal = diagonal(sub)
    tails, rows = [], []
    for k in range(nf):
        tail = codes_ref[k, nl * sub :, :].astype(jnp.float32)
        tails.append(tail * (scale / SPAN))
        row = jnp.where(on_diagonal, tail[nl : nl + 1, :], 0.0)
        rows.append(jnp.sum(row, axis=1, keepdims=True))
    for n in range(nl):
        total = jnp.zeros((sub, LANES), jnp.float32)
        for k in range(nf):
            code = codes_ref[k, n * sub : (n + 1) * sub, :].astype(jnp.float32)
            size = jnp.log(jnp.abs(code)) * (1.0 / math.log(2.0)) + BASE
            size = jnp.where(code < 0, -size, size)
            total += size * tails[k][n : n + 1, :] * rows[k]
        logits_ref[:, n * LANES : (n + 1) * LANES] = total

    logits = logits_ref[...]
    top = jnp.max(logits, axis=1, keepdims=True)
    v = logits - top
    v = v - jnp.log(jnp.sum(jnp.exp(v), axis=1, keepdims=True))
    shift = jnp.max(v, axis=0, keepdims=True)
    kern = lane_blocks(jnp.exp(v - shift).astype(jnp.bfloat16))
    terms = [row for term in split3(shift) for row in lane_blocks(term)]
    tail = stack_rows(terms, KERNEL_TAIL).astype(jnp.bfloat16)
    for z in range(nz):
        for n, part in enumerate(kern):
            out_ref[z, n * sub : (n + 1) * sub, :] = part
        out_ref[z, nl * sub :, :] = tail


def spread(block, axes, n):
    copies = jnp.broadcast_to(block[None], (n,) + block.shape)
    return lax.all_to_all(copies, axes, 0, 0, tiled=True)


def block_shift(ref, z, sub, nl):
    tail = ref[z, nl * sub :, :].astype(jnp.float32)
    return tail[:nl] + tail[nl : 2 * nl] + tail[2 * nl : 3 * nl]


def block_part(ref, z, sub, n):
    return ref[z, n * sub : (n + 1) * sub, :].astype(jnp.float32)


def group_sum(v):
    return functools.reduce(jnp.add, [v[k : k + 8] for k in range(0, v.shape[0], 8)])


def statistics_kernel(sub, own_ref, out_ref):
    nz = own_ref.shape[0]
    nl = out_ref.shape[1]
    shifts = [block_shift(own_ref, z, sub, nl) for z in range(nz)]
    top = functools.reduce(jnp.maximum, shifts)
    total = [jnp.zeros((8, LANES), jnp.float32)] * nl
    for z in range(nz):
        factor = jnp.exp(shifts[z] - top)
        for n in range(nl):
            part = group_sum(block_part(own_ref, z, sub, n))
            total[n] = total[n] + factor[n : n + 1] * part
    total = [jnp.sum(t, axis=0, keepdims=True) for t in total]
    log_sum = top + jnp.log(stack_rows(total, nl))
    out_ref[...] = jnp.broadcast_to(log_sum[None], out_ref.shape)


def columns_kernel(sub, a, stats_ref, own_ref, core_ref, mass_ref, far_ref, col_ref, b_ref, out_ref):
    nz = own_ref.shape[0]
    nl = out_ref.shape[1]
    stats = stats_ref[...]
    far = jnp.max(stats, axis=0)
    b = mass_ref[...] / jnp.sum(mass_ref[...])
    col = b / jnp.sum(jnp.exp(stats - far[None]), axis=0)
    cols = [jnp.zeros((8, LANES), jnp.float32)] * nl
    for z in range(nz):
        for ref in (own_ref, core_ref):
            factor = jnp.exp(block_shift(ref, z, sub, nl) - far) * col
            plan = [block_part(ref, z, sub, n) * factor[n : n + 1] for n in range(nl)]
            row = a / jnp.sum(functools.reduce(jnp.add, plan), axis=1, keepdims=True)
            for n in range(nl):
                cols[n] = cols[n] + group_sum(plan[n] * row)
    cols = [jnp.sum(t, axis=0, keepdims=True) for t in cols]
    far_ref[...] = far
    b_ref[...] = b
    col_ref[...] = col
    out_ref[...] = jnp.broadcast_to(stack_rows(cols, nl)[None], out_ref.shape)


def hold_kernel(in_ref, out_ref):
    out_ref[...] = jnp.zeros_like(out_ref)


def mixture_kernel(
    sub,
    a,
    place_ref,
    sums_ref,
    far_ref,
    col_ref,
    b_ref,
    own_ref,
    core_own_ref,
    other_ref,
    core_other_ref,
    train_ref,
    core_train_ref,
    held_ref,
    out_ref,
    plan_ref,
    blocks_vmem,
    train_vmem,
    sems,
):
    _, nz, _, _ = blocks_vmem.shape
    nl = sums_ref.shape[1]
    nh = nl // 2
    rows = nz * sub
    c, yl = place_ref[0], place_ref[1]
    late = (other_ref, core_other_ref)
    loads = [
        pltpu.make_async_copy(src, blocks_vmem.at[k], sems.at[k])
        for k, src in enumerate(late)
    ]
    sources = (own_ref, core_own_ref, blocks_vmem.at[0], blocks_vmem.at[1])
    copies = [
        pltpu.make_async_copy(src, train_vmem.at[k], sems.at[len(late) + k])
        for k, src in enumerate((train_ref, core_train_ref))
    ]
    for copy in loads + copies:
        copy.start()
    far = far_ref[...]
    col = col_ref[...] * (b_ref[...] / jnp.sum(sums_ref[...], axis=0))

    def step(i, z, cols):
        ref = sources[i]
        factor = jnp.exp(block_shift(ref, z, sub, nl) - far) * col
        plan = [block_part(ref, z, sub, n) * factor[n : n + 1] for n in range(nl)]
        row = a / jnp.sum(functools.reduce(jnp.add, plan), axis=1, keepdims=True)
        side = yl if i < 2 else 1 - yl
        start = pl.multiple_of((i % 2 * 2 + side) * rows + z * sub, sub)
        sums = []
        for n in range(nh):
            part = jnp.where(c == 0, plan[n], plan[nh + n]) * row
            sums.append(cols[n] + group_sum(part))
            lane = n * LANES
            plan_ref[pl.ds(start, sub), lane : lane + LANES] = part.astype(jnp.bfloat16)
        return tuple(sums)

    cols = (jnp.zeros((8, LANES), jnp.float32),) * nh
    for i in range(len(sources)):
        if i >= 2:
            loads[i - 2].wait()
        cols = lax.fori_loop(0, nz, functools.partial(step, i), cols, unroll=2)

    half = nh * LANES
    for copy in copies:
        copy.wait()
    mixed = lax.dot_general(
        plan_ref[...],
        train_vmem[...].reshape(4 * rows, train_ref.shape[1]),
        (((0,), (0,)), ((), ())),
        preferred_element_type=jnp.float32,
    )
    nchips = out_ref.shape[0]
    mine = half // nchips
    parts = lane_blocks(mixed.astype(jnp.bfloat16))
    for n, part in enumerate(parts):
        out_ref[:, n * mine : (n + 1) * mine, :] = part.reshape(nchips, mine, LANES)
    per = LANES // mine
    for n in range(nh):
        total = jnp.sum(cols[n], axis=0, keepdims=True)
        tail = stack_rows(split3(total), MIXTURE_TAIL).astype(jnp.bfloat16)
        out_ref[n * per : (n + 1) * per, len(parts) * mine :, :] = jnp.broadcast_to(
            tail[None], (per, MIXTURE_TAIL, LANES)
        )


def output_kernel(place_ref, got_ref, out_ref):
    mine, feats = out_ref.shape
    nl = feats // LANES
    total = jnp.sum(got_ref[...].astype(jnp.float32), axis=0)
    mass = total[nl * mine : nl * mine + 1] + (
        total[nl * mine + 1 : nl * mine + 2] + total[nl * mine + 2 : nl * mine + 3]
    )
    lane = lax.broadcasted_iota(jnp.int32, (mine, LANES), 1)
    target = lax.broadcasted_iota(jnp.int32, (mine, LANES), 0) + place_ref[2] * mine
    mass = jnp.sum(jnp.where(lane == target, mass, 0.0), axis=1, keepdims=True)
    for n in range(nl):
        part = total[n * mine : (n + 1) * mine] / mass
        out_ref[:, n * LANES : (n + 1) * LANES] = part.astype(jnp.bfloat16)


def shards(train, target, mass):
    rows, feats = train.shape
    nc = lax.axis_size("c")
    nchips = lax.axis_size(CHIPS)
    nex = nc * nchips
    nz = lax.axis_size("z")
    nf = lax.axis_size(FEAT)
    mine = target.shape[0]
    nt = mine * nex
    nl = nt // LANES
    half = nt // nc
    sub = rows // nf
    scale = 3.0 / math.sqrt(F)
    a = 1.0 / (rows * nex)
    full = pl.BlockSpec(memory_space=VMEM)
    anywhere = pl.BlockSpec(memory_space=pl.ANY)
    scalars = pl.BlockSpec(memory_space=pltpu.SMEM)

    core_train = lax.ppermute(train, "c", SWAP)

    same_core = spread(target, CHIPS, nchips).reshape(nchips * mine, feats)
    mass = mass.reshape(lax.axis_size("yh"), lax.axis_size("x"), nc, mine)
    mass = mass.transpose(2, 1, 0, 3).reshape(nl, LANES)
    targets = spread(same_core, "c", nc).reshape(nt, feats)

    codes = pl.pallas_call(
        functools.partial(encode_kernel, sub),
        out_shape=jax.ShapeDtypeStruct((nf, nl * sub + CODE_TAIL, LANES), jnp.bfloat16),
        in_specs=[full] * 2,
        out_specs=full,
        scratch_shapes=[VMEM((2, 4 * sub, nt), jnp.float32)],
        compiler_params=MIDDLE,
    )(train, targets)
    codes = lax.all_to_all(codes, PIECES, 0, 0, tiled=True)
    blocks = pl.pallas_call(
        functools.partial(rows_kernel, sub, scale),
        out_shape=jax.ShapeDtypeStruct((nz, nl * sub + KERNEL_TAIL, LANES), jnp.bfloat16),
        in_specs=[full],
        out_specs=full,
        scratch_shapes=[VMEM((sub, nt), jnp.float32)],
        compiler_params=MIDDLE,
    )(codes)

    own = lax.all_to_all(blocks, "z", 0, 0, tiled=True)
    other = lax.ppermute(own, "yl", SWAP)
    core_own = lax.ppermute(own, "c", SWAP)

    def copies(axes):
        return jax.ShapeDtypeStruct((lax.axis_size(axes), nl, LANES), jnp.float32)

    vector = jax.ShapeDtypeStruct((nl, LANES), jnp.float32)
    stats = pl.pallas_call(
        functools.partial(statistics_kernel, sub),
        out_shape=copies(ROWS),
        in_specs=[full],
        out_specs=full,
        compiler_params=SMALL,
    )(own)
    stats = lax.all_to_all(stats, ROWS, 0, 0, tiled=True)
    far, col, b, sums = pl.pallas_call(
        functools.partial(columns_kernel, sub, a),
        out_shape=(vector, vector, vector, copies(CHIP_ROWS)),
        in_specs=[full] * 4,
        out_specs=(full,) * 4,
        compiler_params=SMALL,
    )(stats, own, core_own, mass)
    sums = lax.all_to_all(sums, CHIP_ROWS, 0, 0, tiled=True)
    held = pl.pallas_call(
        hold_kernel,
        out_shape=jax.ShapeDtypeStruct((8, LANES), jnp.float32),
        in_specs=[anywhere],
        out_specs=full,
        compiler_params=SMALL,
    )(other)
    core_other = lax.ppermute(other, "c", SWAP)

    slot = jnp.bitwise_and(lax.axis_index(CHIPS), LANES // mine - 1)
    place = jnp.stack([lax.axis_index("c"), lax.axis_index("yl"), slot]).astype(jnp.int32)
    block = feats // LANES * mine + MIXTURE_TAIL
    send = pl.pallas_call(
        functools.partial(mixture_kernel, sub, a),
        out_shape=jax.ShapeDtypeStruct((nchips, block, LANES), jnp.bfloat16),
        in_specs=[scalars] + [full] * 6 + [anywhere] * 5,
        out_specs=full,
        scratch_shapes=[
            VMEM((nc * rows, half), jnp.bfloat16),
            VMEM((2,) + own.shape, jnp.bfloat16),
            VMEM((2, rows, feats), jnp.bfloat16),
            pltpu.SemaphoreType.DMA((4,)),
        ],
        compiler_params=LARGE,
    )(place, sums, far, col, b, own, core_own, other, core_other, train, core_train, held)
    got = lax.all_to_all(send, CHIPS, 0, 0, tiled=True)
    return pl.pallas_call(
        output_kernel,
        out_shape=jax.ShapeDtypeStruct((mine, feats), jnp.bfloat16),
        in_specs=[scalars, full],
        out_specs=full,
        compiler_params=SMALL,
    )(place, got)


def solution(mesh):
    fine = Mesh(mesh.devices.reshape(4, 4, 2, 8, 2), ("yh", "x", "c", "z", "yl"))

    return jax.shard_map(
        shards,
        mesh=fine,
        in_specs=(P(EX, FEAT), P(EX, FEAT), P()),
        out_specs=P(EX, FEAT),
        check_vma=False,
    )
```

```python
import functools
import math

import jax
import jax.numpy as jnp
from jax import lax
from jax.experimental import pallas as pl
from jax.experimental.pallas import tpu as pltpu
from jax.sharding import Mesh, PartitionSpec as P


F = 16384
CHIPS = ("x", "yh")
EX = ("yh", "x", "c")
FEAT = ("z", "yl")
PIECES = ("yl", "z")
ROWS = ("x", "yh", "yl", "c")
CHIP_ROWS = ("x", "yh", "yl")
LANES = 128
CODE_TAIL = 8
KERNEL_TAIL = 16
MIXTURE_TAIL = 8
SWAP = [(0, 1), (1, 0)]
VMEM = pltpu.VMEM
MIDDLE = pltpu.CompilerParams(vmem_limit_bytes=12 * 2**20)
SMALL = pltpu.CompilerParams(vmem_limit_bytes=4 * 2**20)
LARGE = pltpu.CompilerParams(vmem_limit_bytes=24 * 2**20)


SPAN = 249.0
BASE = 124.0


def round_up(v):
    return (v * (1.0 + 2.0**-7)).astype(jnp.bfloat16).astype(jnp.float32)


def split3(v):
    hi = v.astype(jnp.bfloat16).astype(jnp.float32)
    mid = (v - hi).astype(jnp.bfloat16).astype(jnp.float32)
    return hi, mid, v - hi - mid


def stack_rows(rows, height):
    index = lax.broadcasted_iota(jnp.int32, (height, LANES), 0)
    out = jnp.zeros((height, LANES), jnp.float32)
    for k, row in enumerate(rows):
        out = jnp.where(index == k, row, out)
    return out


def lane_blocks(v):
    return [v[:, k : k + LANES] for k in range(0, v.shape[1], LANES)]


def diagonal(sub):
    return lax.broadcasted_iota(jnp.int32, (sub, LANES), 0) == (
        lax.broadcasted_iota(jnp.int32, (sub, LANES), 1)
    )


def encode_kernel(sub, train_ref, targets_ref, out_ref, partial_ref):
    rows = train_ref.shape[0]
    step = partial_ref.shape[1]
    on_diagonal = diagonal(sub)
    for start in range(0, rows, step):
        slot = start // step % 2
        partial_ref[slot] = lax.dot_general(
            train_ref[start : start + step, :],
            targets_ref[...],
            (((1,), (1,)), ((), ())),
            preferred_element_type=jnp.float32,
        )
        for j in range(step // sub):
            k = start // sub + j
            p = partial_ref[slot, j * sub : (j + 1) * sub, :]
            high = jnp.max(p, axis=1, keepdims=True)
            low = jnp.min(p, axis=1, keepdims=True)
            p = p - 0.5 * (high + low)
            wide = jnp.max(jnp.abs(p), axis=1, keepdims=True)
            row = round_up(jnp.maximum(wide, 1e-30))
            p = p * (1.0 / row)
            col = round_up(jnp.maximum(jnp.max(jnp.abs(p), axis=0, keepdims=True), 1e-30))
            u = p * (1.0 / col)
            code = jnp.exp2(jnp.abs(u) * SPAN - BASE)
            code = jnp.where(u < 0, -code, code).astype(jnp.bfloat16)
            parts = lane_blocks(code)
            for n, part in enumerate(parts):
                out_ref[k, n * sub : (n + 1) * sub, :] = part
            row = jnp.sum(jnp.where(on_diagonal, row, 0.0), axis=0, keepdims=True)
            tail = stack_rows(lane_blocks(col) + [row], CODE_TAIL)
            out_ref[k, len(parts) * sub :, :] = tail.astype(jnp.bfloat16)


def rows_kernel(sub, scale, codes_ref, out_ref, logits_ref):
    nf = codes_ref.shape[0]
    nz = out_ref.shape[0]
    nl = logits_ref.shape[1] // LANES
    on_diagonal = diagonal(sub)
    tails, rows = [], []
    for k in range(nf):
        tail = codes_ref[k, nl * sub :, :].astype(jnp.float32)
        tails.append(tail * (scale / SPAN))
        row = jnp.where(on_diagonal, tail[nl : nl + 1, :], 0.0)
        rows.append(jnp.sum(row, axis=1, keepdims=True))
    for n in range(nl):
        total = jnp.zeros((sub, LANES), jnp.float32)
        for k in range(nf):
            code = codes_ref[k, n * sub : (n + 1) * sub, :].astype(jnp.float32)
            size = jnp.log(jnp.abs(code)) * (1.0 / math.log(2.0)) + BASE
            size = jnp.where(code < 0, -size, size)
            total += size * tails[k][n : n + 1, :] * rows[k]
        logits_ref[:, n * LANES : (n + 1) * LANES] = total

    logits = logits_ref[...]
    top = jnp.max(logits, axis=1, keepdims=True)
    v = logits - top
    v = v - jnp.log(jnp.sum(jnp.exp(v), axis=1, keepdims=True))
    shift = jnp.max(v, axis=0, keepdims=True)
    kern = lane_blocks(jnp.exp(v - shift).astype(jnp.bfloat16))
    terms = [row for term in split3(shift) for row in lane_blocks(term)]
    tail = stack_rows(terms, KERNEL_TAIL).astype(jnp.bfloat16)
    for z in range(nz):
        for n, part in enumerate(kern):
            out_ref[z, n * sub : (n + 1) * sub, :] = part
        out_ref[z, nl * sub :, :] = tail


def spread(block, axes, n):
    copies = jnp.broadcast_to(block[None], (n,) + block.shape)
    return lax.all_to_all(copies, axes, 0, 0, tiled=True)


def block_shift(ref, z, sub, nl):
    tail = ref[z, nl * sub :, :].astype(jnp.float32)
    return tail[:nl] + tail[nl : 2 * nl] + tail[2 * nl : 3 * nl]


def block_part(ref, z, sub, n):
    return ref[z, n * sub : (n + 1) * sub, :].astype(jnp.float32)


def group_sum(v):
    return functools.reduce(jnp.add, [v[k : k + 8] for k in range(0, v.shape[0], 8)])


def statistics_kernel(sub, own_ref, out_ref):
    nz = own_ref.shape[0]
    nl = out_ref.shape[1]
    shifts = [block_shift(own_ref, z, sub, nl) for z in range(nz)]
    top = functools.reduce(jnp.maximum, shifts)
    total = [jnp.zeros((8, LANES), jnp.float32)] * nl
    for z in range(nz):
        factor = jnp.exp(shifts[z] - top)
        for n in range(nl):
            part = group_sum(block_part(own_ref, z, sub, n))
            total[n] = total[n] + factor[n : n + 1] * part
    total = [jnp.sum(t, axis=0, keepdims=True) for t in total]
    log_sum = top + jnp.log(stack_rows(total, nl))
    out_ref[...] = jnp.broadcast_to(log_sum[None], out_ref.shape)


def columns_kernel(
    sub,
    a,
    stats_ref,
    own_ref,
    core_ref,
    mass_ref,
    far_ref,
    col_ref,
    b_ref,
    out_ref,
    core_vmem,
    sem,
):
    nz = own_ref.shape[0]
    nl = out_ref.shape[1]
    load = pltpu.make_async_copy(core_ref, core_vmem, sem)
    load.start()
    stats = stats_ref[...]
    far = jnp.max(stats, axis=0)
    b = mass_ref[...] / jnp.sum(mass_ref[...])
    col = b / jnp.sum(jnp.exp(stats - far[None]), axis=0)
    cols = [jnp.zeros((8, LANES), jnp.float32)] * nl
    for ref in (own_ref, core_vmem):
        if ref is core_vmem:
            load.wait()
        for z in range(nz):
            factor = jnp.exp(block_shift(ref, z, sub, nl) - far) * col
            plan = [block_part(ref, z, sub, n) * factor[n : n + 1] for n in range(nl)]
            row = a / jnp.sum(functools.reduce(jnp.add, plan), axis=1, keepdims=True)
            for n in range(nl):
                cols[n] = cols[n] + group_sum(plan[n] * row)
    cols = [jnp.sum(t, axis=0, keepdims=True) for t in cols]
    far_ref[...] = far
    b_ref[...] = b
    col_ref[...] = col
    out_ref[...] = jnp.broadcast_to(stack_rows(cols, nl)[None], out_ref.shape)


def hold_kernel(in_ref, out_ref):
    out_ref[...] = jnp.zeros_like(out_ref)


def mixture_kernel(
    sub,
    a,
    place_ref,
    sums_ref,
    far_ref,
    col_ref,
    b_ref,
    own_ref,
    core_own_ref,
    other_ref,
    core_other_ref,
    train_ref,
    core_train_ref,
    held_ref,
    out_ref,
    plan_ref,
    blocks_vmem,
    train_vmem,
    sems,
):
    _, nz, _, _ = blocks_vmem.shape
    nl = sums_ref.shape[1]
    nh = nl // 2
    rows = nz * sub
    c, yl = place_ref[0], place_ref[1]
    late = (core_own_ref, other_ref, core_other_ref)
    loads = [
        pltpu.make_async_copy(src, blocks_vmem.at[k], sems.at[k])
        for k, src in enumerate(late)
    ]
    sources = (own_ref,) + tuple(blocks_vmem.at[k] for k in range(len(late)))
    copies = [
        pltpu.make_async_copy(src, train_vmem.at[k], sems.at[len(late) + k])
        for k, src in enumerate((train_ref, core_train_ref))
    ]
    for copy in loads + copies:
        copy.start()
    far = far_ref[...]
    col = col_ref[...] * (b_ref[...] / jnp.sum(sums_ref[...], axis=0))

    def step(i, z, cols):
        ref = sources[i]
        factor = jnp.exp(block_shift(ref, z, sub, nl) - far) * col
        plan = [block_part(ref, z, sub, n) * factor[n : n + 1] for n in range(nl)]
        row = a / jnp.sum(functools.reduce(jnp.add, plan), axis=1, keepdims=True)
        side = yl if i < 2 else 1 - yl
        start = pl.multiple_of((i % 2 * 2 + side) * rows + z * sub, sub)
        sums = []
        for n in range(nh):
            part = jnp.where(c == 0, plan[n], plan[nh + n]) * row
            sums.append(cols[n] + group_sum(part))
            lane = n * LANES
            plan_ref[pl.ds(start, sub), lane : lane + LANES] = part.astype(jnp.bfloat16)
        return tuple(sums)

    cols = (jnp.zeros((8, LANES), jnp.float32),) * nh
    for i in range(len(sources)):
        if i >= 1:
            loads[i - 1].wait()
        cols = lax.fori_loop(0, nz, functools.partial(step, i), cols, unroll=2)

    half = nh * LANES
    for copy in copies:
        copy.wait()
    mixed = lax.dot_general(
        plan_ref[...],
        train_vmem[...].reshape(4 * rows, train_ref.shape[1]),
        (((0,), (0,)), ((), ())),
        preferred_element_type=jnp.float32,
    )
    nchips = out_ref.shape[0]
    mine = half // nchips
    parts = lane_blocks(mixed.astype(jnp.bfloat16))
    for n, part in enumerate(parts):
        out_ref[:, n * mine : (n + 1) * mine, :] = part.reshape(nchips, mine, LANES)
    per = LANES // mine
    for n in range(nh):
        total = jnp.sum(cols[n], axis=0, keepdims=True)
        tail = stack_rows(split3(total), MIXTURE_TAIL).astype(jnp.bfloat16)
        out_ref[n * per : (n + 1) * per, len(parts) * mine :, :] = jnp.broadcast_to(
            tail[None], (per, MIXTURE_TAIL, LANES)
        )


def output_kernel(place_ref, got_ref, out_ref):
    mine, feats = out_ref.shape
    nl = feats // LANES
    total = jnp.sum(got_ref[...].astype(jnp.float32), axis=0)
    mass = total[nl * mine : nl * mine + 1] + (
        total[nl * mine + 1 : nl * mine + 2] + total[nl * mine + 2 : nl * mine + 3]
    )
    lane = lax.broadcasted_iota(jnp.int32, (mine, LANES), 1)
    target = lax.broadcasted_iota(jnp.int32, (mine, LANES), 0) + place_ref[2] * mine
    mass = jnp.sum(jnp.where(lane == target, mass, 0.0), axis=1, keepdims=True)
    for n in range(nl):
        part = total[n * mine : (n + 1) * mine] / mass
        out_ref[:, n * LANES : (n + 1) * LANES] = part.astype(jnp.bfloat16)


def shards(train, target, mass):
    rows, feats = train.shape
    nc = lax.axis_size("c")
    nchips = lax.axis_size(CHIPS)
    nex = nc * nchips
    nz = lax.axis_size("z")
    nf = lax.axis_size(FEAT)
    mine = target.shape[0]
    nt = mine * nex
    nl = nt // LANES
    half = nt // nc
    sub = rows // nf
    scale = 3.0 / math.sqrt(F)
    a = 1.0 / (rows * nex)
    full = pl.BlockSpec(memory_space=VMEM)
    anywhere = pl.BlockSpec(memory_space=pl.ANY)
    scalars = pl.BlockSpec(memory_space=pltpu.SMEM)

    core_train = lax.ppermute(train, "c", SWAP)

    same_core = spread(target, CHIPS, nchips).reshape(nchips * mine, feats)
    mass = mass.reshape(lax.axis_size("yh"), lax.axis_size("x"), nc, mine)
    mass = mass.transpose(2, 1, 0, 3).reshape(nl, LANES)
    targets = spread(same_core, "c", nc).reshape(nt, feats)

    codes = pl.pallas_call(
        functools.partial(encode_kernel, sub),
        out_shape=jax.ShapeDtypeStruct((nf, nl * sub + CODE_TAIL, LANES), jnp.bfloat16),
        in_specs=[full] * 2,
        out_specs=full,
        scratch_shapes=[VMEM((2, 4 * sub, nt), jnp.float32)],
        compiler_params=MIDDLE,
    )(train, targets)
    codes = lax.all_to_all(codes, PIECES, 0, 0, tiled=True)
    blocks = pl.pallas_call(
        functools.partial(rows_kernel, sub, scale),
        out_shape=jax.ShapeDtypeStruct((nz, nl * sub + KERNEL_TAIL, LANES), jnp.bfloat16),
        in_specs=[full],
        out_specs=full,
        scratch_shapes=[VMEM((sub, nt), jnp.float32)],
        compiler_params=MIDDLE,
    )(codes)

    own = lax.all_to_all(blocks, "z", 0, 0, tiled=True)
    other = lax.ppermute(own, "yl", SWAP)
    core_own = lax.ppermute(own, "c", SWAP)

    def copies(axes):
        return jax.ShapeDtypeStruct((lax.axis_size(axes), nl, LANES), jnp.float32)

    vector = jax.ShapeDtypeStruct((nl, LANES), jnp.float32)
    stats = pl.pallas_call(
        functools.partial(statistics_kernel, sub),
        out_shape=copies(ROWS),
        in_specs=[full],
        out_specs=full,
        compiler_params=SMALL,
    )(own)
    stats = lax.all_to_all(stats, ROWS, 0, 0, tiled=True)
    far, col, b, sums = pl.pallas_call(
        functools.partial(columns_kernel, sub, a),
        out_shape=(vector, vector, vector, copies(CHIP_ROWS)),
        in_specs=[full, full, anywhere, full],
        out_specs=(full,) * 4,
        scratch_shapes=[VMEM(own.shape, jnp.bfloat16), pltpu.SemaphoreType.DMA],
        compiler_params=SMALL,
    )(stats, own, core_own, mass)
    sums = lax.all_to_all(sums, CHIP_ROWS, 0, 0, tiled=True)
    held = pl.pallas_call(
        hold_kernel,
        out_shape=jax.ShapeDtypeStruct((8, LANES), jnp.float32),
        in_specs=[anywhere],
        out_specs=full,
        compiler_params=SMALL,
    )(other)
    core_other = lax.ppermute(other, "c", SWAP)

    slot = jnp.bitwise_and(lax.axis_index(CHIPS), LANES // mine - 1)
    place = jnp.stack([lax.axis_index("c"), lax.axis_index("yl"), slot]).astype(jnp.int32)
    block = feats // LANES * mine + MIXTURE_TAIL
    send = pl.pallas_call(
        functools.partial(mixture_kernel, sub, a),
        out_shape=jax.ShapeDtypeStruct((nchips, block, LANES), jnp.bfloat16),
        in_specs=[scalars] + [full] * 5 + [anywhere] * 6,
        out_specs=full,
        scratch_shapes=[
            VMEM((nc * rows, half), jnp.bfloat16),
            VMEM((3,) + own.shape, jnp.bfloat16),
            VMEM((2, rows, feats), jnp.bfloat16),
            pltpu.SemaphoreType.DMA((5,)),
        ],
        compiler_params=LARGE,
    )(place, sums, far, col, b, own, core_own, other, core_other, train, core_train, held)
    got = lax.all_to_all(send, CHIPS, 0, 0, tiled=True)
    return pl.pallas_call(
        output_kernel,
        out_shape=jax.ShapeDtypeStruct((mine, feats), jnp.bfloat16),
        in_specs=[scalars, full],
        out_specs=full,
        compiler_params=SMALL,
    )(place, got)


def solution(mesh):
    fine = Mesh(mesh.devices.reshape(4, 4, 2, 8, 2), ("yh", "x", "c", "z", "yl"))

    return jax.shard_map(
        shards,
        mesh=fine,
        in_specs=(P(EX, FEAT), P(EX, FEAT), P()),
        out_specs=P(EX, FEAT),
        check_vma=False,
    )
```

```python
import functools
import math

import jax
import jax.numpy as jnp
from jax import lax
from jax.experimental import pallas as pl
from jax.experimental.pallas import tpu as pltpu
from jax.sharding import Mesh, PartitionSpec as P


F = 16384
CHIPS = ("x", "yh")
EX = ("yh", "x", "c")
FEAT = ("z", "yl")
PIECES = ("yl", "z")
ROWS = ("x", "yh", "yl", "c")
LANES = 128
CODE_TAIL = 8
KERNEL_TAIL = 16
MIXTURE_TAIL = 8
SWAP = [(0, 1), (1, 0)]
VMEM = pltpu.VMEM
MIDDLE = pltpu.CompilerParams(vmem_limit_bytes=12 * 2**20)
SMALL = pltpu.CompilerParams(vmem_limit_bytes=4 * 2**20)
LARGE = pltpu.CompilerParams(vmem_limit_bytes=24 * 2**20)


SPAN = 249.0
BASE = 124.0


def round_up(v):
    return (v * (1.0 + 2.0**-7)).astype(jnp.bfloat16).astype(jnp.float32)


def split3(v):
    hi = v.astype(jnp.bfloat16).astype(jnp.float32)
    mid = (v - hi).astype(jnp.bfloat16).astype(jnp.float32)
    return hi, mid, v - hi - mid


def stack_rows(rows, height):
    index = lax.broadcasted_iota(jnp.int32, (height, LANES), 0)
    out = jnp.zeros((height, LANES), jnp.float32)
    for k, row in enumerate(rows):
        out = jnp.where(index == k, row, out)
    return out


def lane_blocks(v):
    return [v[:, k : k + LANES] for k in range(0, v.shape[1], LANES)]


def diagonal(sub):
    return lax.broadcasted_iota(jnp.int32, (sub, LANES), 0) == (
        lax.broadcasted_iota(jnp.int32, (sub, LANES), 1)
    )


def encode_kernel(sub, train_ref, targets_ref, out_ref, partial_ref):
    rows = train_ref.shape[0]
    step = partial_ref.shape[1]
    on_diagonal = diagonal(sub)
    for start in range(0, rows, step):
        slot = start // step % 2
        partial_ref[slot] = lax.dot_general(
            train_ref[start : start + step, :],
            targets_ref[...],
            (((1,), (1,)), ((), ())),
            preferred_element_type=jnp.float32,
        )
        for j in range(step // sub):
            k = start // sub + j
            p = partial_ref[slot, j * sub : (j + 1) * sub, :]
            high = jnp.max(p, axis=1, keepdims=True)
            low = jnp.min(p, axis=1, keepdims=True)
            p = p - 0.5 * (high + low)
            wide = jnp.max(jnp.abs(p), axis=1, keepdims=True)
            row = round_up(jnp.maximum(wide, 1e-30))
            p = p * (1.0 / row)
            col = round_up(jnp.maximum(jnp.max(jnp.abs(p), axis=0, keepdims=True), 1e-30))
            u = p * (1.0 / col)
            code = jnp.exp2(jnp.abs(u) * SPAN - BASE)
            code = jnp.where(u < 0, -code, code).astype(jnp.bfloat16)
            parts = lane_blocks(code)
            for n, part in enumerate(parts):
                out_ref[k, n * sub : (n + 1) * sub, :] = part
            row = jnp.sum(jnp.where(on_diagonal, row, 0.0), axis=0, keepdims=True)
            tail = stack_rows(lane_blocks(col) + [row], CODE_TAIL)
            out_ref[k, len(parts) * sub :, :] = tail.astype(jnp.bfloat16)


def rows_kernel(sub, scale, codes_ref, out_ref, logits_ref):
    nf = codes_ref.shape[0]
    nz = out_ref.shape[0]
    nl = logits_ref.shape[1] // LANES
    on_diagonal = diagonal(sub)
    tails, rows = [], []
    for k in range(nf):
        tail = codes_ref[k, nl * sub :, :].astype(jnp.float32)
        tails.append(tail * (scale / SPAN))
        row = jnp.where(on_diagonal, tail[nl : nl + 1, :], 0.0)
        rows.append(jnp.sum(row, axis=1, keepdims=True))
    for n in range(nl):
        total = jnp.zeros((sub, LANES), jnp.float32)
        for k in range(nf):
            code = codes_ref[k, n * sub : (n + 1) * sub, :].astype(jnp.float32)
            size = jnp.log(jnp.abs(code)) * (1.0 / math.log(2.0)) + BASE
            size = jnp.where(code < 0, -size, size)
            total += size * tails[k][n : n + 1, :] * rows[k]
        logits_ref[:, n * LANES : (n + 1) * LANES] = total

    logits = logits_ref[...]
    top = jnp.max(logits, axis=1, keepdims=True)
    v = logits - top
    v = v - jnp.log(jnp.sum(jnp.exp(v), axis=1, keepdims=True))
    shift = jnp.max(v, axis=0, keepdims=True)
    kern = lane_blocks(jnp.exp(v - shift).astype(jnp.bfloat16))
    terms = [row for term in split3(shift) for row in lane_blocks(term)]
    tail = stack_rows(terms, KERNEL_TAIL).astype(jnp.bfloat16)
    for z in range(nz):
        for n, part in enumerate(kern):
            out_ref[z, n * sub : (n + 1) * sub, :] = part
        out_ref[z, nl * sub :, :] = tail


def spread(block, axes, n):
    copies = jnp.broadcast_to(block[None], (n,) + block.shape)
    return lax.all_to_all(copies, axes, 0, 0, tiled=True)


def block_shift(ref, z, sub, nl):
    tail = ref[z, nl * sub :, :].astype(jnp.float32)
    return tail[:nl] + tail[nl : 2 * nl] + tail[2 * nl : 3 * nl]


def block_part(ref, z, sub, n):
    return ref[z, n * sub : (n + 1) * sub, :].astype(jnp.float32)


def group_sum(v):
    return functools.reduce(jnp.add, [v[k : k + 8] for k in range(0, v.shape[0], 8)])


def statistics_kernel(sub, own_ref, out_ref):
    nz = own_ref.shape[0]
    nl = out_ref.shape[1]
    shifts = [block_shift(own_ref, z, sub, nl) for z in range(nz)]
    top = functools.reduce(jnp.maximum, shifts)
    total = [jnp.zeros((8, LANES), jnp.float32)] * nl
    for z in range(nz):
        factor = jnp.exp(shifts[z] - top)
        for n in range(nl):
            part = group_sum(block_part(own_ref, z, sub, n))
            total[n] = total[n] + factor[n : n + 1] * part
    total = [jnp.sum(t, axis=0, keepdims=True) for t in total]
    log_sum = top + jnp.log(stack_rows(total, nl))
    out_ref[...] = jnp.broadcast_to(log_sum[None], out_ref.shape)


def columns_kernel(sub, a, stats_ref, own_ref, mass_ref, far_ref, col_ref, b_ref, out_ref):
    nz = own_ref.shape[0]
    nl = out_ref.shape[1]
    stats = stats_ref[...]
    far = jnp.max(stats, axis=0)
    b = mass_ref[...] / jnp.sum(mass_ref[...])
    col = b / jnp.sum(jnp.exp(stats - far[None]), axis=0)
    cols = [jnp.zeros((8, LANES), jnp.float32)] * nl
    for z in range(nz):
        factor = jnp.exp(block_shift(own_ref, z, sub, nl) - far) * col
        plan = [block_part(own_ref, z, sub, n) * factor[n : n + 1] for n in range(nl)]
        row = a / jnp.sum(functools.reduce(jnp.add, plan), axis=1, keepdims=True)
        for n in range(nl):
            cols[n] = cols[n] + group_sum(plan[n] * row)
    cols = [jnp.sum(t, axis=0, keepdims=True) for t in cols]
    far_ref[...] = far
    b_ref[...] = b
    col_ref[...] = col
    out_ref[...] = jnp.broadcast_to(stack_rows(cols, nl)[None], out_ref.shape)


def hold_kernel(in_ref, out_ref):
    out_ref[...] = jnp.zeros_like(out_ref)


def mixture_kernel(
    sub,
    a,
    place_ref,
    sums_ref,
    far_ref,
    col_ref,
    b_ref,
    own_ref,
    core_own_ref,
    other_ref,
    core_other_ref,
    train_ref,
    core_train_ref,
    held_ref,
    out_ref,
    plan_ref,
    blocks_vmem,
    train_vmem,
    sems,
):
    _, nz, _, _ = blocks_vmem.shape
    nl = sums_ref.shape[1]
    nh = nl // 2
    rows = nz * sub
    c, yl = place_ref[0], place_ref[1]
    late = (core_own_ref, other_ref, core_other_ref)
    loads = [
        pltpu.make_async_copy(src, blocks_vmem.at[k], sems.at[k])
        for k, src in enumerate(late)
    ]
    sources = (own_ref,) + tuple(blocks_vmem.at[k] for k in range(len(late)))
    copies = [
        pltpu.make_async_copy(src, train_vmem.at[k], sems.at[len(late) + k])
        for k, src in enumerate((train_ref, core_train_ref))
    ]
    for copy in loads + copies:
        copy.start()
    far = far_ref[...]
    col = col_ref[...] * (b_ref[...] / jnp.sum(sums_ref[...], axis=0))

    def step(i, z, cols):
        ref = sources[i]
        factor = jnp.exp(block_shift(ref, z, sub, nl) - far) * col
        plan = [block_part(ref, z, sub, n) * factor[n : n + 1] for n in range(nl)]
        row = a / jnp.sum(functools.reduce(jnp.add, plan), axis=1, keepdims=True)
        side = yl if i < 2 else 1 - yl
        start = pl.multiple_of((i % 2 * 2 + side) * rows + z * sub, sub)
        sums = []
        for n in range(nh):
            part = jnp.where(c == 0, plan[n], plan[nh + n]) * row
            sums.append(cols[n] + group_sum(part))
            lane = n * LANES
            plan_ref[pl.ds(start, sub), lane : lane + LANES] = part.astype(jnp.bfloat16)
        return tuple(sums)

    cols = (jnp.zeros((8, LANES), jnp.float32),) * nh
    for i in range(len(sources)):
        if i >= 1:
            loads[i - 1].wait()
        cols = lax.fori_loop(0, nz, functools.partial(step, i), cols, unroll=2)

    half = nh * LANES
    for copy in copies:
        copy.wait()
    mixed = lax.dot_general(
        plan_ref[...],
        train_vmem[...].reshape(4 * rows, train_ref.shape[1]),
        (((0,), (0,)), ((), ())),
        preferred_element_type=jnp.float32,
    )
    nchips = out_ref.shape[0]
    mine = half // nchips
    parts = lane_blocks(mixed.astype(jnp.bfloat16))
    for n, part in enumerate(parts):
        out_ref[:, n * mine : (n + 1) * mine, :] = part.reshape(nchips, mine, LANES)
    per = LANES // mine
    for n in range(nh):
        total = jnp.sum(cols[n], axis=0, keepdims=True)
        tail = stack_rows(split3(total), MIXTURE_TAIL).astype(jnp.bfloat16)
        out_ref[n * per : (n + 1) * per, len(parts) * mine :, :] = jnp.broadcast_to(
            tail[None], (per, MIXTURE_TAIL, LANES)
        )


def output_kernel(place_ref, got_ref, out_ref):
    mine, feats = out_ref.shape
    nl = feats // LANES
    total = jnp.sum(got_ref[...].astype(jnp.float32), axis=0)
    mass = total[nl * mine : nl * mine + 1] + (
        total[nl * mine + 1 : nl * mine + 2] + total[nl * mine + 2 : nl * mine + 3]
    )
    lane = lax.broadcasted_iota(jnp.int32, (mine, LANES), 1)
    target = lax.broadcasted_iota(jnp.int32, (mine, LANES), 0) + place_ref[2] * mine
    mass = jnp.sum(jnp.where(lane == target, mass, 0.0), axis=1, keepdims=True)
    for n in range(nl):
        part = total[n * mine : (n + 1) * mine] / mass
        out_ref[:, n * LANES : (n + 1) * LANES] = part.astype(jnp.bfloat16)


def shards(train, target, mass):
    rows, feats = train.shape
    nc = lax.axis_size("c")
    nchips = lax.axis_size(CHIPS)
    nex = nc * nchips
    nz = lax.axis_size("z")
    nf = lax.axis_size(FEAT)
    mine = target.shape[0]
    nt = mine * nex
    nl = nt // LANES
    half = nt // nc
    sub = rows // nf
    scale = 3.0 / math.sqrt(F)
    a = 1.0 / (rows * nex)
    full = pl.BlockSpec(memory_space=VMEM)
    anywhere = pl.BlockSpec(memory_space=pl.ANY)
    scalars = pl.BlockSpec(memory_space=pltpu.SMEM)

    core_train = lax.ppermute(train, "c", SWAP)

    same_core = spread(target, CHIPS, nchips).reshape(nchips * mine, feats)
    mass = mass.reshape(lax.axis_size("yh"), lax.axis_size("x"), nc, mine)
    mass = mass.transpose(2, 1, 0, 3).reshape(nl, LANES)
    targets = spread(same_core, "c", nc).reshape(nt, feats)

    codes = pl.pallas_call(
        functools.partial(encode_kernel, sub),
        out_shape=jax.ShapeDtypeStruct((nf, nl * sub + CODE_TAIL, LANES), jnp.bfloat16),
        in_specs=[full] * 2,
        out_specs=full,
        scratch_shapes=[VMEM((2, 8 * sub, nt), jnp.float32)],
        compiler_params=MIDDLE,
    )(train, targets)
    codes = lax.all_to_all(codes, PIECES, 0, 0, tiled=True)
    blocks = pl.pallas_call(
        functools.partial(rows_kernel, sub, scale),
        out_shape=jax.ShapeDtypeStruct((nz, nl * sub + KERNEL_TAIL, LANES), jnp.bfloat16),
        in_specs=[full],
        out_specs=full,
        scratch_shapes=[VMEM((sub, nt), jnp.float32)],
        compiler_params=MIDDLE,
    )(codes)

    own = lax.all_to_all(blocks, "z", 0, 0, tiled=True)
    other = lax.ppermute(own, "yl", SWAP)
    core_own = lax.ppermute(own, "c", SWAP)

    def copies(axes):
        return jax.ShapeDtypeStruct((lax.axis_size(axes), nl, LANES), jnp.float32)

    vector = jax.ShapeDtypeStruct((nl, LANES), jnp.float32)
    stats = pl.pallas_call(
        functools.partial(statistics_kernel, sub),
        out_shape=copies(ROWS),
        in_specs=[full],
        out_specs=full,
        compiler_params=SMALL,
    )(own)
    stats = lax.all_to_all(stats, ROWS, 0, 0, tiled=True)
    far, col, b, sums = pl.pallas_call(
        functools.partial(columns_kernel, sub, a),
        out_shape=(vector, vector, vector, copies(ROWS)),
        in_specs=[full] * 3,
        out_specs=(full,) * 4,
        compiler_params=SMALL,
    )(stats, own, mass)
    sums = lax.all_to_all(sums, ROWS, 0, 0, tiled=True)
    held = pl.pallas_call(
        hold_kernel,
        out_shape=jax.ShapeDtypeStruct((8, LANES), jnp.float32),
        in_specs=[anywhere],
        out_specs=full,
        compiler_params=SMALL,
    )(other)
    core_other = lax.ppermute(other, "c", SWAP)

    slot = jnp.bitwise_and(lax.axis_index(CHIPS), LANES // mine - 1)
    place = jnp.stack([lax.axis_index("c"), lax.axis_index("yl"), slot]).astype(jnp.int32)
    block = feats // LANES * mine + MIXTURE_TAIL
    send = pl.pallas_call(
        functools.partial(mixture_kernel, sub, a),
        out_shape=jax.ShapeDtypeStruct((nchips, block, LANES), jnp.bfloat16),
        in_specs=[scalars] + [full] * 5 + [anywhere] * 6,
        out_specs=full,
        scratch_shapes=[
            VMEM((nc * rows, half), jnp.bfloat16),
            VMEM((3,) + own.shape, jnp.bfloat16),
            VMEM((2, rows, feats), jnp.bfloat16),
            pltpu.SemaphoreType.DMA((5,)),
        ],
        compiler_params=LARGE,
    )(place, sums, far, col, b, own, core_own, other, core_other, train, core_train, held)
    got = lax.all_to_all(send, CHIPS, 0, 0, tiled=True)
    return pl.pallas_call(
        output_kernel,
        out_shape=jax.ShapeDtypeStruct((mine, feats), jnp.bfloat16),
        in_specs=[scalars, full],
        out_specs=full,
        compiler_params=SMALL,
    )(place, got)


def solution(mesh):
    fine = Mesh(mesh.devices.reshape(4, 4, 2, 8, 2), ("yh", "x", "c", "z", "yl"))

    return jax.shard_map(
        shards,
        mesh=fine,
        in_specs=(P(EX, FEAT), P(EX, FEAT), P()),
        out_specs=P(EX, FEAT),
        check_vma=False,
    )
```
